256 devices in a mesh: group: 8 (over y, z_hi), tp: 32 (over x, z_lo, core).
Axes of the slice: x: 4, y: 4, z: 8 (z_hi: 2, z_lo: 4; z = z_hi * 4 + z_lo), core: 2. Of those that a mesh axis runs over, the one named last changes fastest.
Arguments:
- queries: bfloat16 [8, 8, 2, 8192], P('group', None, None, 'tp'), may hold values from -24 to 24
- new_keys: bfloat16 [8, 8, 2, 1024], P('group', None, None, 'tp'), may hold values from -16 to 16
- new_values: bfloat16 [8, 8, 2, 1024], P('group', None, None, 'tp'), may hold values from -24 to 24
- key_pages: bfloat16 [8, 2048, 16, 1024], P('group', 'tp'), may hold values from -16 to 16
- value_pages: bfloat16 [8, 2048, 16, 1024], P('group', 'tp'), may hold values from -24 to 24
- page_owner: int32 [8, 2048], P('group', 'tp'), may hold values from 0 to 8, as said below
- page_fill: int32 [8, 2048], P('group', 'tp'), may hold values from 0 to 16, as said below
- target_slot: int32 [8, 8], P('group'), may hold values from 0 to 8, as said below
- out_weight: bfloat16 [8192, 8192], P(None, 'tp'), may hold values from -0.0625 to 0.0625
Outputs:
- projected: bfloat16 [8, 8, 2, 8192], P('group', None, None, 'tp')
The draws below stay inside these ranges and needn't reach their ends.
Inputs may be any that keep to these rules, and one draw needn't show every extreme that they name: `page_owner`: the owning request slot, or 8 for a free page. Of each pair of groups g and g XOR (4) one is loaded (no free pages) and the other light; group 0 is light, and so is group 8 - 1 when 8 > 2. One device holds at most 16 pages of moving requests, and some device of every loaded group holds exactly 16. `page_fill`: 1 to 16 for a used page, 0 for a free one. `target_slot`: 8 for a request that stays. Every group has exactly one moving request; their slots in the partner group are distinct and own no pages there.
All inputs are finite; a program needn't handle non-finite values.
Results may differ from the reference program's by a relative error of at most 0.0065.
Values may be sent and summed in bfloat16 or wider, within the bound.
A program may use at most 64 MiB of HBM per device.

```python
import math
import jax
import jax.numpy as jnp
from jax import lax

D = 8192
HEADS = 64
KVH = 8
HD = 128
PAGE = 16
STEPS = 2
CAP = 16
REQ = 8
PAGES_DEV = 64
MOVE = 1
GROUPS = 8
POOL = 2048


def distinct_order(key, shape):
    raw = jax.random.randint(key, shape, 0, 1 << 20)
    ranks = raw * shape[-1] + jnp.arange(shape[-1], dtype=jnp.int32)
    return jnp.argsort(ranks, axis=-1).astype(jnp.int32)


def layout(key):
    base = jax.random.fold_in(key, 4242)
    streams = jax.random.split(base, 11)
    half = GROUPS // 2
    tp_count = POOL // PAGES_DEV
    group_ids = jnp.arange(GROUPS, dtype=jnp.int32)
    pair_ids = group_ids % half
    partner_ids = jnp.bitwise_xor(group_ids, half).astype(jnp.int32)
    low_side = group_ids < half
    low_loaded = jax.random.randint(streams[0], (half,), 0, 2) == 1
    pair_range = jnp.arange(half, dtype=jnp.int32)
    low_loaded = jnp.where(pair_range == half - 1, True, low_loaded)
    low_loaded = jnp.where(pair_range == 0, False, low_loaded)
    loaded = jnp.where(low_side, low_loaded[pair_ids], jnp.logical_not(low_loaded[pair_ids]))
    orders = distinct_order(streams[1], (GROUPS, REQ))
    slot_ids = jnp.arange(REQ, dtype=jnp.int32)
    matched = (orders[:, :MOVE, None] == slot_ids[None, None, :]).astype(jnp.int32)
    receiving = orders[partner_ids][:, MOVE:2 * MOVE]
    slot_table = (REQ + jnp.sum(matched * (receiving[:, :, None] - REQ), axis=1)).astype(jnp.int32)
    device_shape = (GROUPS, tp_count, PAGES_DEV)
    position = jnp.arange(PAGES_DEV, dtype=jnp.int32)[None, None, :]
    mover_count = jax.random.randint(streams[3], (GROUPS, tp_count, 1), (CAP + 1) // 2, CAP + 1)
    full_device = jax.random.randint(streams[4], (GROUPS, 1, 1), 0, tp_count)
    mover_count = jnp.where(jnp.arange(tp_count, dtype=jnp.int32)[None, :, None] == full_device, CAP, mover_count)
    pick_mover = jax.random.randint(streams[5], device_shape, 0, MOVE)
    pick_stay = jax.random.randint(streams[6], device_shape, 2 * MOVE, REQ)
    rows = jnp.broadcast_to(orders[:, None, :], (GROUPS, tp_count, REQ))
    mover_owner = jnp.take_along_axis(rows, pick_mover, axis=2)
    stay_owner = jnp.take_along_axis(rows, pick_stay, axis=2)
    loaded_owner = jnp.where(position < mover_count, mover_owner, stay_owner)
    light_count = jax.random.randint(streams[7], (GROUPS, tp_count, 1), max(PAGES_DEV // 4, 1), PAGES_DEV // 2 + 1)
    light_owner = jnp.where(position < light_count, loaded_owner, REQ)
    owner_table = jnp.where(loaded[:, None, None], loaded_owner, light_owner)
    shuffle = distinct_order(streams[8], device_shape)
    owner_table = jnp.take_along_axis(owner_table, shuffle, axis=2).astype(jnp.int32)
    partial_fill = jax.random.randint(streams[9], device_shape, 1, PAGE + 1)
    partial_on = jax.random.randint(streams[10], device_shape, 0, 4) == 0
    fill_table = jnp.where(owner_table < REQ, jnp.where(partial_on, partial_fill, PAGE), 0).astype(jnp.int32)
    return (owner_table.reshape(GROUPS, POOL), fill_table.reshape(GROUPS, POOL), slot_table)


def draw_page_owner(key, part):
    return layout(key)[0]


def draw_page_fill(key, part):
    return layout(key)[1]


def draw_target_slot(key, part):
    return layout(key)[2]


def sign_table(key):
    signs = jax.random.randint(jax.random.fold_in(key, 777), (KVH, HD), 0, 2)
    return (2 * signs - 1).astype(jnp.float32)


def draw_queries(key, part):
    streams = jax.random.split(jax.random.fold_in(key, 101), 3)
    shape = (GROUPS, REQ, STEPS, HEADS, HD)
    flag_shape = (GROUPS, REQ, STEPS, HEADS, 1)
    noise = 1.5 * jax.random.truncated_normal(streams[0], -6.0, 6.0, shape, jnp.float32)
    aligned = jax.random.randint(streams[1], flag_shape, 0, 4) == 0
    levels = jnp.array([3.0, 5.0, 7.0], jnp.float32)
    strength = jnp.take(levels, jax.random.randint(streams[2], flag_shape, 0, 3))
    head_signs = jnp.repeat(sign_table(key), HEADS // KVH, axis=0)
    planted = strength * head_signs + 0.5 * noise
    result = jnp.where(aligned, planted, noise)
    return result.reshape(GROUPS, REQ, STEPS, D).astype(jnp.bfloat16)


def planted_keys(key, lead_shape, salt, shown_rate):
    streams = jax.random.split(jax.random.fold_in(key, salt), 3)
    full_shape = lead_shape + (KVH, HD)
    flag_shape = lead_shape + (KVH, 1)
    noise = jax.random.truncated_normal(streams[0], -6.0, 6.0, full_shape, jnp.float32)
    chosen = jax.random.randint(streams[1], flag_shape, 0, shown_rate) == 0
    reach = jax.random.uniform(streams[2], flag_shape, jnp.float32, 1.5, 3.5)
    planted = reach * sign_table(key) + 0.5 * noise
    result = jnp.where(chosen, planted, noise)
    return result.reshape(lead_shape + (KVH * HD,)).astype(jnp.bfloat16)


def draw_key_pages(key, part):
    return planted_keys(key, (GROUPS, POOL, PAGE), 202, 64)


def draw_new_keys(key, part):
    return planted_keys(key, (GROUPS, REQ, STEPS), 303, 2)


def block_scale(key, shape, shards, low, high):
    def one(axis_at, blocks):
        steps = jax.random.uniform(jax.random.fold_in(jax.random.fold_in(key, 6), axis_at), (blocks,), jnp.float32, low / len(shards), high / len(shards))
        return jnp.repeat(jnp.exp(steps), shape[axis_at] // blocks).reshape((-1,) + (1,) * (len(shape) - axis_at - 1))

    level = one(*shards[0])
    for cut in shards[1:]:
        level = level * one(*cut)
    return level


def gaussian(key, extent, width, most, cuts=(), kind=jnp.bfloat16):
    entries = jax.random.normal(key, extent, jnp.float32) * width
    if len(cuts) > 0:
        entries = block_scale(key, extent, cuts, -0.22, 0.18) * entries
    return jnp.clip(entries, min=-most, max=most).astype(kind)


def setup_inputs(seed: int = 0) -> dict:
    key_list = jax.random.split(jax.random.key(seed), 10)
    queries = draw_queries(jax.random.fold_in(key_list[9], 71), 0)
    new_keys = draw_new_keys(jax.random.fold_in(key_list[9], 71), 0)
    new_values = gaussian(key_list[2], (GROUPS, REQ, STEPS, KVH * HD), 4.0, 24.0, ((0, 8), (3, 32)))
    key_pages = draw_key_pages(jax.random.fold_in(key_list[9], 71), 0)
    value_pages = gaussian(key_list[4], (GROUPS, POOL, PAGE, KVH * HD), 4.0, 24.0, ((0, 8), (1, 32)))
    page_owner = draw_page_owner(jax.random.fold_in(key_list[9], 71), 0)
    page_fill = draw_page_fill(jax.random.fold_in(key_list[9], 71), 0)
    target_slot = draw_target_slot(jax.random.fold_in(key_list[9], 71), 0)
    out_weight = gaussian(key_list[8], (D, D), D ** -0.5, 0.0625, ((1, 32),))
    return dict(queries=queries, new_keys=new_keys, new_values=new_values, key_pages=key_pages, value_pages=value_pages, page_owner=page_owner, page_fill=page_fill, target_slot=target_slot, out_weight=out_weight)


neg_big = -1e+30

def merge_states(first, second):
    largest = jnp.maximum(first[0], second[0])
    scale_first = jnp.exp(first[0] - largest)
    scale_second = jnp.exp(second[0] - largest)
    return (largest, first[1] * scale_first + second[1] * scale_second, first[2] * scale_first[..., None] + second[2] * scale_second[..., None])

def page_states(query_rows, key_block, value_block, owner_rows, fill_counts, row_count):
    page_count = key_block.shape[0]
    step_count = query_rows.shape[1]
    group_size = HEADS // KVH
    scale_factor = 1.0 / math.sqrt(HD)
    clipped = jnp.clip(owner_rows, 0, row_count - 1).astype(jnp.int32)
    query_page = jnp.take(query_rows, clipped, axis=0).reshape(page_count, step_count, KVH, group_size, HD).astype(jnp.float32)
    key_page = key_block.reshape(page_count, PAGE, KVH, HD).astype(jnp.float32)
    value_page = value_block.reshape(page_count, PAGE, KVH, HD).astype(jnp.float32)
    scores = jnp.einsum('psgjd,ptgd->psgjt', query_page, key_page) * scale_factor
    live_token = (owner_rows < row_count)[:, None] & (lax.broadcasted_iota(jnp.int32, (page_count, PAGE), 1) < fill_counts[:, None])
    token_mask = live_token[:, None, None, None, :]
    scores = jnp.where(token_mask, scores, neg_big)
    page_top = lax.optimization_barrier(jnp.max(scores, axis=4)).reshape(page_count, step_count * HEADS)
    member = owner_rows[None, :] == lax.broadcasted_iota(jnp.int32, (row_count, page_count), 0)
    row_top = lax.optimization_barrier(jnp.max(jnp.where(member[:, :, None], page_top[None], neg_big), axis=1))
    top_page = jnp.take(row_top, clipped, axis=0).reshape(page_count, step_count, KVH, group_size, 1)
    weights = jnp.where(token_mask, jnp.exp(scores - top_page), 0.0).astype(jnp.bfloat16).astype(jnp.float32)
    weighted = jnp.einsum('psgjt,ptgd->psgjd', weights, value_page).reshape(page_count, step_count, HEADS, HD)
    weight_sum = lax.optimization_barrier(jnp.sum(weights, axis=4)).reshape(page_count, step_count, HEADS)
    row_sum = jax.ops.segment_sum(weight_sum, owner_rows, num_segments=row_count + 1)[:row_count]
    row_acc = jax.ops.segment_sum(weighted, owner_rows, num_segments=row_count + 1)[:row_count]
    return (row_top.reshape(row_count, step_count, HEADS), row_sum, row_acc)

def new_token_states(query_heads, key_rows, value_rows, head_kv):
    row_count = key_rows.shape[0]
    step_count = key_rows.shape[1]
    scale_factor = 1.0 / math.sqrt(HD)
    key_heads = jnp.take(key_rows.reshape(row_count, step_count, KVH, HD), head_kv, axis=2).astype(jnp.float32)
    value_heads = jnp.take(value_rows.reshape(row_count, step_count, KVH, HD), head_kv, axis=2).astype(jnp.float32)
    scores = jnp.einsum('rshd,ruhd->rshu', query_heads.astype(jnp.float32), key_heads) * scale_factor
    causal = (lax.broadcasted_iota(jnp.int32, (step_count, step_count), 1) <= lax.broadcasted_iota(jnp.int32, (step_count, step_count), 0))[None, :, None, :]
    scores = jnp.where(causal, scores, neg_big)
    largest = lax.optimization_barrier(jnp.max(scores, axis=3))
    weights = jnp.where(causal, jnp.exp(scores - largest[..., None]), 0.0)
    return (largest, lax.optimization_barrier(jnp.sum(weights, axis=3)), jnp.einsum('rshu,ruhd->rshd', weights, value_heads))

def flatten_rows(member_array):
    return member_array.reshape((member_array.shape[0] * member_array.shape[1],) + member_array.shape[2:])

def reference(queries, new_keys, new_values, key_pages, value_pages, page_owner, page_fill, target_slot, out_weight):
    groups = queries.shape[0]
    row_count = queries.shape[1]
    step_count = queries.shape[2]
    partner = jnp.bitwise_xor(jnp.arange(groups, dtype=jnp.int32), groups // 2).astype(jnp.int32)

    def per_group(group_index):
        owners = page_owner[group_index]
        slot_targets = target_slot[group_index]
        clipped = jnp.clip(owners, 0, row_count - 1).astype(jnp.int32)
        page_target = jnp.take(slot_targets, clipped)
        occupied = owners < row_count
        moving = occupied & (page_target < row_count)
        local_rows = jnp.where(occupied, jnp.where(moving, row_count + page_target, owners), 2 * row_count).astype(jnp.int32)
        query_rows = jnp.concatenate([queries[group_index], queries[partner[group_index]]], axis=0)
        return page_states(query_rows, key_pages[group_index], value_pages[group_index], local_rows, page_fill[group_index], 2 * row_count)
    all_states = lax.map(per_group, jnp.arange(groups, dtype=jnp.int32))
    own_part = tuple((member_array[:, :row_count] for member_array in all_states))
    arrived = tuple((member_array[partner][:, row_count:] for member_array in all_states))
    cache_state = merge_states(own_part, arrived)
    cache_flat = tuple((flatten_rows(member_array) for member_array in cache_state))
    head_kv = (jnp.arange(HEADS, dtype=jnp.int32) // (HEADS // KVH)).astype(jnp.int32)
    query_heads = flatten_rows(queries).reshape(groups * row_count, step_count, HEADS, HD)
    new_terms = new_token_states(query_heads, flatten_rows(new_keys), flatten_rows(new_values), head_kv)
    finished = merge_states(cache_flat, new_terms)
    attention = (finished[2] / finished[1][..., None]).astype(jnp.bfloat16).reshape(groups * row_count * step_count, HEADS * HD)
    projected = jnp.dot(attention, out_weight, preferred_element_type=jnp.float32).astype(jnp.bfloat16)
    return projected.reshape(groups, row_count, step_count, HEADS * HD)
```

```python
import functools
import math

import jax
import jax.numpy as jnp
from jax import lax
from jax.experimental import pallas as pl
from jax.experimental.pallas import tpu as pltpu
from jax.sharding import PartitionSpec as P

HD = 128
PAGE = 16
NZ = 4
NEG = -1e30
C2 = math.log2(math.e) / math.sqrt(HD)
MESH = pl.DeviceIdType.MESH
F32 = jnp.float32
BF16 = jnp.bfloat16


def iota(shape, dim):
    return lax.broadcasted_iota(jnp.int32, shape, dim)


def kernel(
    groups,
    nx,
    q_ref,
    nkv_ref,
    owner_ref,
    fill_ref,
    slot_ref,
    k_hbm,
    v_hbm,
    w_hbm,
    out_ref,
    k_ref,
    v_ref,
    w_ref,
    bias_ref,
    line_ref,
    part_ref,
    sib_ref,
    qall_ref,
    aout_ref,
    arecv_ref,
    stat_ref,
    sout_ref,
    srecv_ref,
    zacc_ref,
    zstat_ref,
    pout_ref,
    psout_ref,
    pacc_ref,
    pstat_ref,
    att_ref,
    load_sem,
    l_send,
    l_recv,
    p_send,
    p_recv,
    s_send,
    s_recv,
    q_send,
    q_recv,
    a_send,
    a_recv,
    t_send,
    t_recv,
    z_send,
    z_recv,
    y_send,
    y_recv,
    m_send,
    m_recv,
    n_send,
    n_recv,
    o_send,
    o_recv,
):
    np_ = nx * 2
    tokens = k_ref.shape[0]
    pages = owner_ref.shape[1]
    g = lax.axis_index("group")
    t = lax.axis_index("tp")
    x = lax.div(t, 8)
    z = lax.rem(lax.div(t, 2), NZ)
    c = lax.rem(t, 2)
    pp = x * 2 + c
    partner = lax.rem(g + groups // 2, groups)

    def on_plane(k):
        other = lax.rem(pp + k, np_)
        return other, (g, lax.div(other, 2) * 8 + z * 2 + lax.rem(other, 2))

    def on_line(group, k):
        other = lax.rem(z + k, NZ)
        return other, (group, x * 8 + other * 2 + c)

    def remote(src, dst, send, recv, device):
        return pltpu.make_async_remote_copy(
            src_ref=src,
            dst_ref=dst,
            send_sem=send,
            recv_sem=recv,
            device_id=device,
            device_id_type=MESH,
        )

    sent = []

    def send(*args):
        copy = remote(*args)
        copy.start()
        sent.append(copy)

    loads = [
        pltpu.make_async_copy(k_hbm, k_ref, load_sem.at[0]),
        pltpu.make_async_copy(v_hbm, v_ref, load_sem.at[1]),
        pltpu.make_async_copy(w_hbm, w_ref, load_sem.at[2]),
    ]
    for load in loads:
        load.start()

    barrier = pltpu.get_barrier_semaphore()
    greeted = 0
    for k in range(NZ):
        pl.semaphore_signal(barrier, inc=1, device_id=on_line(partner, k)[1], device_id_type=MESH)
        greeted += 1
    for k in range(1, NZ):
        pl.semaphore_signal(barrier, inc=1, device_id=on_line(g, k)[1], device_id_type=MESH)
        greeted += 1
    for k in range(1, np_):
        pl.semaphore_signal(barrier, inc=1, device_id=on_plane(k)[1], device_id_type=MESH)
        greeted += 1

    place = (iota((32, HD), 1) == iota((32, HD), 0) + 32 * lax.rem(t, 4)).astype(BF16)
    line_ref[z, 0:2] = q_ref[...]
    line_ref[z, 2] = jnp.dot(nkv_ref[0], place, preferred_element_type=F32).astype(BF16)
    line_ref[z, 3] = jnp.dot(nkv_ref[1], place, preferred_element_type=F32).astype(BF16)

    owned = jnp.where(
        jnp.broadcast_to(owner_ref[...], (8, pages)) == iota((8, pages), 0),
        jnp.broadcast_to(fill_ref[...], (8, pages)),
        0,
    )
    spread = (lax.div(iota((pages, tokens), 1), PAGE) == iota((pages, tokens), 0)).astype(BF16)
    held = jnp.dot(owned.astype(F32).astype(BF16), spread, preferred_element_type=F32)
    within = lax.rem(iota((8, tokens), 1), PAGE).astype(F32)
    bias_ref[...] = jnp.where(within < held, 0.0, NEG)

    slots = [slot_ref[0, r] for r in range(8)]
    row16 = lax.rem(iota((16, 32), 0), 8)
    target = jnp.full((16, 32), 8, jnp.int32)
    for r in range(8):
        target = jnp.where(row16 == r, slots[r], target)
    col = iota((16, 32), 1)
    step_row = lax.div(iota((16, 32), 0), 8)
    from_own = (target == 8) & (col == iota((16, 32), 0))
    from_other = (target < 8) & (col == 16 + step_row * 8 + target)
    pick = (from_own | from_other).astype(BF16)

    pl.semaphore_wait(barrier, greeted)

    for k in range(NZ):
        send(
            line_ref.at[z, 0:2], part_ref.at[z], p_send.at[k], p_recv.at[z], on_line(partner, k)[1]
        )
    for k in range(1, NZ):
        send(line_ref.at[z], line_ref.at[z], l_send.at[k], l_recv.at[z], on_line(g, k)[1])
    for k in range(1, NZ):
        other, device = on_line(g, k)
        remote(line_ref.at[z], line_ref.at[other], l_send.at[k], l_recv.at[other], device).wait_recv()
    for k in range(NZ):
        other, device = on_line(partner, k)
        remote(
            line_ref.at[z, 0:2], part_ref.at[other], p_send.at[k], p_recv.at[other], device
        ).wait_recv()

    for i in range(NZ):
        for e in range(2):
            both = jnp.concatenate([line_ref[i, e], part_ref[i, e]], axis=0)
            qall_ref[pp, i, e] = jnp.dot(pick, both, preferred_element_type=F32).astype(BF16)
    for k in range(1, np_):
        send(qall_ref.at[pp], qall_ref.at[pp], q_send.at[k], q_recv.at[pp], on_plane(k)[1])
    sibling = (g, x * 8 + z * 2 + (1 - c))
    send(line_ref.at[:, 2:4], sib_ref, s_send, s_recv, sibling)

    loads[0].wait()
    loads[1].wait()
    lane = iota((HD, HD), 1)
    stat_ref[...] = jnp.zeros((HD, HD), F32)
    for k in range(nx):
        xk = lax.rem(x + k, nx)
        for cc in range(2) if k else (1 - c,):
            other = xk * 2 + cc
            remote(
                qall_ref.at[pp], qall_ref.at[other], q_send.at[0], q_recv.at[other], sibling
            ).wait_recv()
        tops, sums = [], []
        for b in range(2):
            columns = pl.ds(pl.multiple_of((xk * 2 + b) * HD, HD), HD)
            query = jnp.concatenate(
                [qall_ref[xk * 2 + cc, 2 * b : 2 * b + 2].reshape(64, HD) for cc in range(2)], axis=0
            )
            score = lax.dot_general(
                query, k_ref[:, columns], (((1,), (1,)), ((), ())), preferred_element_type=F32
            )
            score = (score.reshape(16, 8, tokens) + bias_ref[...][None]).reshape(HD, tokens)
            top = jnp.max(score, axis=1, keepdims=True)
            weight = jnp.exp2((score - top) * C2)
            total = jnp.sum(weight, axis=1, keepdims=True)
            acc = jnp.dot(weight.astype(BF16), v_ref[:, columns], preferred_element_type=F32)
            acc = acc.astype(BF16)
            for cc in range(2):
                aout_ref[k, cc, b] = acc[cc * 64 : cc * 64 + 64]
            tops.append(top)
            sums.append(total)
        stat = stat_ref[...]
        for cc in range(2):
            part = slice(cc * 64, cc * 64 + 64)
            top = jnp.concatenate([tops[0][part], tops[1][part]], axis=0)
            total = jnp.concatenate([sums[0][part], sums[1][part]], axis=0)
            at = (k * 2 + cc) * 8
            stat = jnp.where(lane == at, top, jnp.where(lane == at + 1, total, stat))
        stat_ref[...] = stat
        for cc in range(2) if k else (1 - c,):
            device = (g, xk * 8 + z * 2 + cc)
            at = k * 2 + cc
            send(aout_ref.at[k, cc], arecv_ref.at[pp], a_send.at[at], a_recv.at[pp], device)
    turned = stat_ref[...].T
    for k in range(nx):
        for cc in range(2):
            at = k * 2 + cc
            sout_ref[at] = turned[at * 8 : at * 8 + 8]
    for k in range(nx):
        xk = lax.rem(x + k, nx)
        for cc in range(2) if k else (1 - c,):
            device = (g, xk * 8 + z * 2 + cc)
            at = k * 2 + cc
            send(sout_ref.at[at], srecv_ref.at[pp], t_send.at[at], t_recv.at[pp], device)
    arecv_ref[pp] = aout_ref[0, c]
    srecv_ref[pp] = sout_ref[c]

    remote(line_ref.at[:, 2:4], sib_ref, s_send, s_recv, sibling).wait_recv()
    tops, sums, news = [], [], []
    late = lax.rem(iota((8, 8, HD), 0), 2) == 1
    for b in range(2):
        new = [
            sum(
                line_ref[2 * b + i, 2 + kv].astype(F32) + sib_ref[2 * b + i, kv].astype(F32)
                for i in range(2)
            )
            for kv in range(2)
        ]
        query = line_ref[2 * b : 2 * b + 2, 0:2].astype(F32).reshape(8, 8, HD)
        first = jnp.sum(query * new[0][0:8][None], axis=2, keepdims=True)
        second = jnp.sum(query * new[0][8:16][None], axis=2, keepdims=True)
        first = jnp.broadcast_to(first, (8, 8, HD))
        second = jnp.where(late, jnp.broadcast_to(second, (8, 8, HD)), NEG)
        top = jnp.maximum(first, second)
        first = jnp.exp2((first - top) * C2)
        second = jnp.exp2((second - top) * C2)
        tops.append(top.reshape(64, HD))
        sums.append((first + second).reshape(64, HD))
        news.append((first * new[1][0:8][None] + second * new[1][8:16][None]).reshape(64, HD))
    new_acc = jnp.concatenate(news, axis=0)
    new_stat = jnp.where(
        lane == 0,
        jnp.concatenate(tops, axis=0),
        jnp.where(lane == 1, jnp.concatenate(sums, axis=0), 0.0),
    ).T
    new_top, new_sum = new_stat[0:1], new_stat[1:2]

    for k in range(1, np_):
        other, device = on_plane(k)
        remote(
            sout_ref.at[0], srecv_ref.at[other], t_send.at[0], t_recv.at[other], device
        ).wait_recv()
    tops = jnp.concatenate([srecv_ref[i, 0:1] for i in range(np_)], axis=0)
    sums = jnp.concatenate([srecv_ref[i, 1:2] for i in range(np_)], axis=0)
    top8 = jnp.max(tops, axis=0, keepdims=True)
    scale = jnp.exp2((tops - top8) * C2)
    sum8 = jnp.sum(scale * sums, axis=0, keepdims=True)
    scale = scale.T
    for k in range(1, np_):
        other, device = on_plane(k)
        remote(
            aout_ref.at[0, 0], arecv_ref.at[other], a_send.at[0], a_recv.at[other], device
        ).wait_recv()
    acc = jnp.zeros((HD, HD), F32)
    for i in range(np_):
        acc += scale[:, i : i + 1] * arecv_ref[i].reshape(HD, HD).astype(F32)
    acc = acc.astype(BF16)
    zacc_ref[z] = acc
    sub = iota((8, HD), 0)

    row = iota((16, HD), 1)
    at = lax.rem(row, 8)
    moves = jnp.zeros((16, HD), jnp.int32)
    for r in range(8):
        moves = jnp.where((at == r) & (slots[r] < 8), 1, moves)
    take = ((moves == 1) & (lax.div(row, 8) == iota((16, HD), 0))).astype(BF16)
    pout_ref[...] = jnp.dot(take, acc, preferred_element_type=F32).astype(BF16)
    moves = moves[0:8] == 1
    zstat_ref[z] = jnp.where(sub == 0, jnp.where(moves, NEG, top8), jnp.where(sub == 1, sum8, 0.0))
    goal = jnp.int32(8)
    for r in range(8):
        goal = jnp.where(slots[r] < 8, slots[r], goal)
    stat = jnp.where(sub == 0, top8, sum8)
    stat = jnp.where(moves, stat, NEG)
    within8 = lax.rem(iota((8, HD), 1), 8)
    for step in (1, 2, 4):
        low = lax.rem(lax.div(within8, step), 2) == 0
        swapped = jnp.where(low, pltpu.roll(stat, HD - step, 1), pltpu.roll(stat, step, 1))
        stat = jnp.maximum(stat, swapped)
    psout_ref[...] = jnp.where(within8 == goal, stat, jnp.where(sub == 0, NEG, 0.0))

    for k in range(NZ):
        device = on_line(partner, k)[1]
        send(pout_ref, pacc_ref.at[z], m_send.at[k], m_recv.at[z], device)
        send(psout_ref, pstat_ref.at[z], n_send.at[k], n_recv.at[z], device)
    for k in range(1, NZ):
        device = on_line(g, k)[1]
        send(zstat_ref.at[z], zstat_ref.at[z], y_send.at[k], y_recv.at[z], device)
        send(zacc_ref.at[z], zacc_ref.at[z], z_send.at[k], z_recv.at[z], device)
    for k in range(1, NZ):
        other, device = on_line(g, k)
        remote(
            zstat_ref.at[z], zstat_ref.at[other], y_send.at[k], y_recv.at[other], device
        ).wait_recv()
        remote(
            zacc_ref.at[z], zacc_ref.at[other], z_send.at[k], z_recv.at[other], device
        ).wait_recv()
    for k in range(NZ):
        other, device = on_line(partner, k)
        remote(pout_ref, pacc_ref.at[other], m_send.at[k], m_recv.at[other], device).wait_recv()
        remote(psout_ref, pstat_ref.at[other], n_send.at[k], n_recv.at[other], device).wait_recv()

    tops = jnp.concatenate(
        [zstat_ref[i, 0:1] for i in range(NZ)] + [pstat_ref[i, 0:1] for i in range(NZ)], axis=0
    )
    sums = jnp.concatenate(
        [zstat_ref[i, 1:2] for i in range(NZ)] + [pstat_ref[i, 1:2] for i in range(NZ)], axis=0
    )
    top = jnp.maximum(jnp.max(tops, axis=0, keepdims=True), new_top)
    scale = jnp.exp2((tops - top) * C2)
    new_scale = jnp.exp2((new_top - top) * C2)
    denominator = jnp.sum(scale * sums, axis=0, keepdims=True) + new_scale * new_sum
    scale = (scale / denominator).T
    new_scale = jnp.broadcast_to(new_scale / denominator, (8, HD)).T
    acc = new_scale[:, 0:1] * new_acc
    for i in range(NZ):
        acc += scale[:, i : i + 1] * zacc_ref[i].astype(F32)
        moved = jnp.broadcast_to(pacc_ref[i].astype(F32)[:, None, :], (16, 8, HD)).reshape(HD, HD)
        acc += scale[:, NZ + i : NZ + i + 1] * moved
    att_ref[pp] = acc.astype(BF16)
    for k in range(1, np_):
        send(att_ref.at[pp], att_ref.at[pp], o_send.at[k], o_recv.at[pp], on_plane(k)[1])

    loads[2].wait()
    result = jnp.zeros((16, out_ref.shape[1]), F32)
    for k in range(np_):
        other, device = on_plane(k)
        if k:
            remote(
                att_ref.at[pp], att_ref.at[other], o_send.at[k], o_recv.at[other], device
            ).wait_recv()
        block = att_ref[other]
        for i in range(NZ):
            at = lax.div(other, 2) * 8 + i * 2 + lax.rem(other, 2)
            rows = pl.ds(pl.multiple_of(at * 256, 256), 256)
            both = jnp.concatenate(
                [block[i * 32 : i * 32 + 16], block[i * 32 + 16 : i * 32 + 32]], axis=1
            )
            result += jnp.dot(both, w_ref[rows, :], preferred_element_type=F32)
    out_ref[...] = result.astype(BF16)
    for copy in sent:
        copy.wait_send()


def solution(mesh):
    groups, tp = mesh.shape["group"], mesh.shape["tp"]
    nx = tp // 8

    def per_device(queries, new_keys, new_values, key_pages, value_pages, owner, fill, slots, weight):
        tokens = key_pages.shape[1] * PAGE
        width = key_pages.shape[3]
        features, columns = weight.shape
        query = queries[0].reshape(8, 2, 2, HD).transpose(2, 1, 0, 3).reshape(2, 16, HD)
        new = jnp.stack([new_keys[0], new_values[0]]).transpose(0, 2, 1, 3).reshape(2, 16, 32)
        vmem = pl.BlockSpec(memory_space=pltpu.VMEM)
        smem = pl.BlockSpec(memory_space=pltpu.SMEM)
        hbm = pl.BlockSpec(memory_space=pl.ANY)
        np_ = 2 * nx
        dma = pltpu.SemaphoreType.DMA
        out = pl.pallas_call(
            functools.partial(kernel, groups, nx),
            out_shape=jax.ShapeDtypeStruct((16, columns), BF16),
            in_specs=[vmem, vmem, vmem, vmem, smem, hbm, hbm, hbm],
            out_specs=vmem,
            scratch_shapes=[
                pltpu.VMEM((tokens, width), BF16),
                pltpu.VMEM((tokens, width), BF16),
                pltpu.VMEM((features, columns), BF16),
                pltpu.VMEM((8, tokens), F32),
                pltpu.VMEM((NZ, 4, 16, HD), BF16),
                pltpu.VMEM((NZ, 2, 16, HD), BF16),
                pltpu.VMEM((NZ, 2, 16, HD), BF16),
                pltpu.VMEM((np_, NZ, 2, 16, HD), BF16),
                pltpu.VMEM((nx, 2, 2, 64, HD), BF16),
                pltpu.VMEM((np_, 2, 64, HD), BF16),
                pltpu.VMEM((HD, HD), F32),
                pltpu.VMEM((np_, 8, HD), F32),
                pltpu.VMEM((np_, 8, HD), F32),
                pltpu.VMEM((NZ, HD, HD), BF16),
                pltpu.VMEM((NZ, 8, HD), F32),
                pltpu.VMEM((16, HD), BF16),
                pltpu.VMEM((8, HD), F32),
                pltpu.VMEM((NZ, 16, HD), BF16),
                pltpu.VMEM((NZ, 8, HD), F32),
                pltpu.VMEM((np_, HD, HD), BF16),
                dma((3,)),
                dma((NZ,)),
                dma((NZ,)),
                dma((NZ,)),
                dma((NZ,)),
                dma,
                dma,
                dma((np_,)),
                dma((np_,)),
                dma((np_,)),
                dma((np_,)),
                dma((np_,)),
                dma((np_,)),
                dma((NZ,)),
                dma((NZ,)),
                dma((NZ,)),
                dma((NZ,)),
                dma((NZ,)),
                dma((NZ,)),
                dma((NZ,)),
                dma((NZ,)),
                dma((np_,)),
                dma((np_,)),
            ],
            compiler_params=pltpu.CompilerParams(
                collective_id=0, has_side_effects=True, vmem_limit_bytes=48 << 20
            ),
        )(
            query,
            new,
            owner,
            fill,
            slots,
            key_pages[0].reshape(tokens, width),
            value_pages[0].reshape(tokens, width),
            weight,
        )
        return out.reshape(2, 8, columns).transpose(1, 0, 2)[None]

    placed = (
        P("group", None, None, "tp"),
        P("group", None, None, "tp"),
        P("group", None, None, "tp"),
        P("group", "tp", None, None),
        P("group", "tp", None, None),
        P("group", "tp"),
        P("group", "tp"),
        P("group", None),
        P(None, "tp"),
    )
    return jax.shard_map(
        per_device,
        mesh=mesh,
        in_specs=placed,
        out_specs=P("group", None, None, "tp"),
        check_vma=False,
    )
```

```python
import functools
import math

import jax
import jax.numpy as jnp
from jax import lax
from jax.experimental import pallas as pl
from jax.experimental.pallas import tpu as pltpu
from jax.sharding import PartitionSpec as P

HD = 128
PAGE = 16
NZ = 4
NEG = -1e30
C2 = math.log2(math.e) / math.sqrt(HD)
MESH = pl.DeviceIdType.MESH
F32 = jnp.float32
BF16 = jnp.bfloat16


def iota(shape, dim):
    return lax.broadcasted_iota(jnp.int32, shape, dim)


def kernel(
    groups,
    nx,
    q_hbm,
    nk_hbm,
    nv_hbm,
    k_hbm,
    v_hbm,
    owner_hbm,
    fill_hbm,
    slot_hbm,
    w_hbm,
    out_ref,
    q_ref,
    nk_ref,
    nv_ref,
    owner_ref,
    fill_ref,
    slot_ref,
    k_ref,
    v_ref,
    w_ref,
    bias_ref,
    line_ref,
    part_ref,
    sib_ref,
    qall_ref,
    aout_ref,
    arecv_ref,
    stat_ref,
    sout_ref,
    srecv_ref,
    zacc_ref,
    zstat_ref,
    pout_ref,
    psout_ref,
    pacc_ref,
    pstat_ref,
    att_ref,
    load_sem,
    l_send,
    l_recv,
    p_send,
    p_recv,
    s_send,
    s_recv,
    q_send,
    q_recv,
    a_send,
    a_recv,
    t_send,
    t_recv,
    z_send,
    z_recv,
    y_send,
    y_recv,
    m_send,
    m_recv,
    n_send,
    n_recv,
    o_send,
    o_recv,
):
    np_ = nx * 2
    tokens = k_ref.shape[0]
    pages = owner_ref.shape[1]
    g = lax.axis_index("group")
    t = lax.axis_index("tp")
    x = lax.div(t, 8)
    z = lax.rem(lax.div(t, 2), NZ)
    c = lax.rem(t, 2)
    pp = x * 2 + c
    partner = lax.rem(g + groups // 2, groups)

    def on_plane(k):
        other = lax.rem(pp + k, np_)
        return other, (g, lax.div(other, 2) * 8 + z * 2 + lax.rem(other, 2))

    def on_line(group, k):
        other = lax.rem(z + k, NZ)
        return other, (group, x * 8 + other * 2 + c)

    def remote(src, dst, send, recv, device):
        return pltpu.make_async_remote_copy(
            src_ref=src,
            dst_ref=dst,
            send_sem=send,
            recv_sem=recv,
            device_id=device,
            device_id_type=MESH,
        )

    sent = []

    def send(*args):
        copy = remote(*args)
        copy.start()
        sent.append(copy)

    def fetch(src, dst, at):
        copy = pltpu.make_async_copy(src, dst, load_sem.at[at])
        copy.start()
        return copy

    small = [
        fetch(q_hbm.at[0], q_ref, 3),
        fetch(nk_hbm.at[0], nk_ref, 4),
        fetch(nv_hbm.at[0], nv_ref, 5),
        fetch(owner_hbm, owner_ref, 6),
        fetch(fill_hbm, fill_ref, 7),
        fetch(slot_hbm, slot_ref, 8),
    ]
    barrier = pltpu.get_barrier_semaphore()
    greeted = 0
    for k in range(NZ):
        pl.semaphore_signal(barrier, inc=1, device_id=on_line(partner, k)[1], device_id_type=MESH)
        greeted += 1
    for k in range(1, NZ):
        pl.semaphore_signal(barrier, inc=1, device_id=on_line(g, k)[1], device_id_type=MESH)
        greeted += 1
    for k in range(1, np_):
        pl.semaphore_signal(barrier, inc=1, device_id=on_plane(k)[1], device_id_type=MESH)
        greeted += 1
    loads = [fetch(k_hbm, k_ref, 0), fetch(v_hbm, v_ref, 1), fetch(w_hbm, w_ref, 2)]
    for copy in small:
        copy.wait()

    place = (iota((32, HD), 1) == iota((32, HD), 0) + 32 * lax.rem(t, 4)).astype(BF16)
    order = (
        iota((16, 16), 1)
        == 2 * lax.rem(iota((16, 16), 0), 8) + lax.div(iota((16, 16), 0), 8)
    ).astype(BF16)

    def by_step(ref):
        rows = ref[...].reshape(16, ref.shape[2])
        return jnp.dot(order, rows, preferred_element_type=F32).astype(BF16)

    query = by_step(q_ref)
    line_ref[z, 0] = query[:, :HD]
    line_ref[z, 1] = query[:, HD:]
    line_ref[z, 2] = jnp.dot(by_step(nk_ref), place, preferred_element_type=F32).astype(BF16)
    line_ref[z, 3] = jnp.dot(by_step(nv_ref), place, preferred_element_type=F32).astype(BF16)

    owned = jnp.where(
        jnp.broadcast_to(owner_ref[...], (8, pages)) == iota((8, pages), 0),
        jnp.broadcast_to(fill_ref[...], (8, pages)),
        0,
    )
    spread = (lax.div(iota((pages, tokens), 1), PAGE) == iota((pages, tokens), 0)).astype(BF16)
    held = jnp.dot(owned.astype(F32).astype(BF16), spread, preferred_element_type=F32)
    within = lax.rem(iota((8, tokens), 1), PAGE).astype(F32)
    bias_ref[...] = jnp.where(within < held, 0.0, NEG)

    slots = [slot_ref[0, r] for r in range(8)]
    row16 = lax.rem(iota((16, 32), 0), 8)
    target = jnp.full((16, 32), 8, jnp.int32)
    for r in range(8):
        target = jnp.where(row16 == r, slots[r], target)
    col = iota((16, 32), 1)
    step_row = lax.div(iota((16, 32), 0), 8)
    from_own = (target == 8) & (col == iota((16, 32), 0))
    from_other = (target < 8) & (col == 16 + step_row * 8 + target)
    pick = (from_own | from_other).astype(BF16)

    pl.semaphore_wait(barrier, greeted)

    for k in range(NZ):
        send(
            line_ref.at[z, 0:2], part_ref.at[z], p_send.at[k], p_recv.at[z], on_line(partner, k)[1]
        )
    for k in range(1, NZ):
        send(line_ref.at[z], line_ref.at[z], l_send.at[k], l_recv.at[z], on_line(g, k)[1])
    for k in range(1, NZ):
        other, device = on_line(g, k)
        remote(line_ref.at[z], line_ref.at[other], l_send.at[k], l_recv.at[other], device).wait_recv()
    for k in range(NZ):
        other, device = on_line(partner, k)
        remote(
            line_ref.at[z, 0:2], part_ref.at[other], p_send.at[k], p_recv.at[other], device
        ).wait_recv()

    for i in range(NZ):
        for e in range(2):
            both = jnp.concatenate([line_ref[i, e], part_ref[i, e]], axis=0)
            qall_ref[pp, i, e] = jnp.dot(pick, both, preferred_element_type=F32).astype(BF16)
    for k in range(1, np_):
        send(qall_ref.at[pp], qall_ref.at[pp], q_send.at[k], q_recv.at[pp], on_plane(k)[1])
    sibling = (g, x * 8 + z * 2 + (1 - c))
    send(line_ref.at[:, 2:4], sib_ref, s_send, s_recv, sibling)

    loads[0].wait()
    loads[1].wait()
    lane = iota((HD, HD), 1)
    stat_ref[...] = jnp.zeros((HD, HD), F32)
    for k in range(nx):
        xk = lax.rem(x + k, nx)
        for cc in range(2) if k else (1 - c,):
            other = xk * 2 + cc
            remote(
                qall_ref.at[pp], qall_ref.at[other], q_send.at[0], q_recv.at[other], sibling
            ).wait_recv()
        tops, sums = [], []
        for b in range(2):
            columns = pl.ds(pl.multiple_of((xk * 2 + b) * HD, HD), HD)
            query = jnp.concatenate(
                [qall_ref[xk * 2 + cc, 2 * b : 2 * b + 2].reshape(64, HD) for cc in range(2)], axis=0
            )
            score = lax.dot_general(
                query, k_ref[:, columns], (((1,), (1,)), ((), ())), preferred_element_type=F32
            )
            score = (score.reshape(16, 8, tokens) + bias_ref[...][None]).reshape(HD, tokens)
            top = jnp.max(score, axis=1, keepdims=True)
            weight = jnp.exp2((score - top) * C2)
            total = jnp.sum(weight, axis=1, keepdims=True)
            acc = jnp.dot(weight.astype(BF16), v_ref[:, columns], preferred_element_type=F32)
            acc = acc.astype(BF16)
            for cc in range(2):
                aout_ref[k, cc, b] = acc[cc * 64 : cc * 64 + 64]
            tops.append(top)
            sums.append(total)
        stat = stat_ref[...]
        for cc in range(2):
            part = slice(cc * 64, cc * 64 + 64)
            top = jnp.concatenate([tops[0][part], tops[1][part]], axis=0)
            total = jnp.concatenate([sums[0][part], sums[1][part]], axis=0)
            at = (k * 2 + cc) * 8
            stat = jnp.where(lane == at, top, jnp.where(lane == at + 1, total, stat))
        stat_ref[...] = stat
        for cc in range(2) if k else (1 - c,):
            device = (g, xk * 8 + z * 2 + cc)
            at = k * 2 + cc
            send(aout_ref.at[k, cc], arecv_ref.at[pp], a_send.at[at], a_recv.at[pp], device)
    turned = stat_ref[...].T
    for k in range(nx):
        for cc in range(2):
            at = k * 2 + cc
            sout_ref[at] = turned[at * 8 : at * 8 + 8]
    for k in range(nx):
        xk = lax.rem(x + k, nx)
        for cc in range(2) if k else (1 - c,):
            device = (g, xk * 8 + z * 2 + cc)
            at = k * 2 + cc
            send(sout_ref.at[at], srecv_ref.at[pp], t_send.at[at], t_recv.at[pp], device)
    arecv_ref[pp] = aout_ref[0, c]
    srecv_ref[pp] = sout_ref[c]

    remote(line_ref.at[:, 2:4], sib_ref, s_send, s_recv, sibling).wait_recv()
    tops, sums, news = [], [], []
    late = lax.rem(iota((8, 8, HD), 0), 2) == 1
    for b in range(2):
        new = [
            sum(
                line_ref[2 * b + i, 2 + kv].astype(F32) + sib_ref[2 * b + i, kv].astype(F32)
                for i in range(2)
            )
            for kv in range(2)
        ]
        query = line_ref[2 * b : 2 * b + 2, 0:2].astype(F32).reshape(8, 8, HD)
        first = jnp.sum(query * new[0][0:8][None], axis=2, keepdims=True)
        second = jnp.sum(query * new[0][8:16][None], axis=2, keepdims=True)
        first = jnp.broadcast_to(first, (8, 8, HD))
        second = jnp.where(late, jnp.broadcast_to(second, (8, 8, HD)), NEG)
        top = jnp.maximum(first, second)
        first = jnp.exp2((first - top) * C2)
        second = jnp.exp2((second - top) * C2)
        tops.append(top.reshape(64, HD))
        sums.append((first + second).reshape(64, HD))
        news.append((first * new[1][0:8][None] + second * new[1][8:16][None]).reshape(64, HD))
    new_acc = jnp.concatenate(news, axis=0)
    new_stat = jnp.where(
        lane == 0,
        jnp.concatenate(tops, axis=0),
        jnp.where(lane == 1, jnp.concatenate(sums, axis=0), 0.0),
    ).T
    new_top, new_sum = new_stat[0:1], new_stat[1:2]

    for k in range(1, np_):
        other, device = on_plane(k)
        remote(
            sout_ref.at[0], srecv_ref.at[other], t_send.at[0], t_recv.at[other], device
        ).wait_recv()
    tops = jnp.concatenate([srecv_ref[i, 0:1] for i in range(np_)], axis=0)
    sums = jnp.concatenate([srecv_ref[i, 1:2] for i in range(np_)], axis=0)
    top8 = jnp.max(tops, axis=0, keepdims=True)
    scale = jnp.exp2((tops - top8) * C2)
    sum8 = jnp.sum(scale * sums, axis=0, keepdims=True)
    scale = scale.T
    for k in range(1, np_):
        other, device = on_plane(k)
        remote(
            aout_ref.at[0, 0], arecv_ref.at[other], a_send.at[0], a_recv.at[other], device
        ).wait_recv()
    acc = jnp.zeros((HD, HD), F32)
    for i in range(np_):
        acc += scale[:, i : i + 1] * arecv_ref[i].reshape(HD, HD).astype(F32)
    acc = acc.astype(BF16)
    zacc_ref[z] = acc
    sub = iota((8, HD), 0)

    row = iota((16, HD), 1)
    at = lax.rem(row, 8)
    moves = jnp.zeros((16, HD), jnp.int32)
    for r in range(8):
        moves = jnp.where((at == r) & (slots[r] < 8), 1, moves)
    take = ((moves == 1) & (lax.div(row, 8) == iota((16, HD), 0))).astype(BF16)
    pout_ref[...] = jnp.dot(take, acc, preferred_element_type=F32).astype(BF16)
    moves = moves[0:8] == 1
    zstat_ref[z] = jnp.where(sub == 0, jnp.where(moves, NEG, top8), jnp.where(sub == 1, sum8, 0.0))
    goal = jnp.int32(8)
    for r in range(8):
        goal = jnp.where(slots[r] < 8, slots[r], goal)
    stat = jnp.where(sub == 0, top8, sum8)
    stat = jnp.where(moves, stat, NEG)
    within8 = lax.rem(iota((8, HD), 1), 8)
    for step in (1, 2, 4):
        low = lax.rem(lax.div(within8, step), 2) == 0
        swapped = jnp.where(low, pltpu.roll(stat, HD - step, 1), pltpu.roll(stat, step, 1))
        stat = jnp.maximum(stat, swapped)
    psout_ref[...] = jnp.where(within8 == goal, stat, jnp.where(sub == 0, NEG, 0.0))

    for k in range(NZ):
        device = on_line(partner, k)[1]
        send(pout_ref, pacc_ref.at[z], m_send.at[k], m_recv.at[z], device)
        send(psout_ref, pstat_ref.at[z], n_send.at[k], n_recv.at[z], device)
    for k in range(1, NZ):
        device = on_line(g, k)[1]
        send(zstat_ref.at[z], zstat_ref.at[z], y_send.at[k], y_recv.at[z], device)
        send(zacc_ref.at[z], zacc_ref.at[z], z_send.at[k], z_recv.at[z], device)
    for k in range(1, NZ):
        other, device = on_line(g, k)
        remote(
            zstat_ref.at[z], zstat_ref.at[other], y_send.at[k], y_recv.at[other], device
        ).wait_recv()
        remote(
            zacc_ref.at[z], zacc_ref.at[other], z_send.at[k], z_recv.at[other], device
        ).wait_recv()
    for k in range(NZ):
        other, device = on_line(partner, k)
        remote(pout_ref, pacc_ref.at[other], m_send.at[k], m_recv.at[other], device).wait_recv()
        remote(psout_ref, pstat_ref.at[other], n_send.at[k], n_recv.at[other], device).wait_recv()

    tops = jnp.concatenate(
        [zstat_ref[i, 0:1] for i in range(NZ)] + [pstat_ref[i, 0:1] for i in range(NZ)], axis=0
    )
    sums = jnp.concatenate(
        [zstat_ref[i, 1:2] for i in range(NZ)] + [pstat_ref[i, 1:2] for i in range(NZ)], axis=0
    )
    top = jnp.maximum(jnp.max(tops, axis=0, keepdims=True), new_top)
    scale = jnp.exp2((tops - top) * C2)
    new_scale = jnp.exp2((new_top - top) * C2)
    denominator = jnp.sum(scale * sums, axis=0, keepdims=True) + new_scale * new_sum
    scale = (scale / denominator).T
    new_scale = jnp.broadcast_to(new_scale / denominator, (8, HD)).T
    acc = new_scale[:, 0:1] * new_acc
    for i in range(NZ):
        acc += scale[:, i : i + 1] * zacc_ref[i].astype(F32)
        moved = jnp.broadcast_to(pacc_ref[i].astype(F32)[:, None, :], (16, 8, HD)).reshape(HD, HD)
        acc += scale[:, NZ + i : NZ + i + 1] * moved
    att_ref[pp] = acc.astype(BF16)
    for k in range(1, np_):
        send(att_ref.at[pp], att_ref.at[pp], o_send.at[k], o_recv.at[pp], on_plane(k)[1])

    loads[2].wait()
    result = jnp.zeros((16, out_ref.shape[1]), F32)
    for k in range(np_):
        other, device = on_plane(k)
        if k:
            remote(
                att_ref.at[pp], att_ref.at[other], o_send.at[k], o_recv.at[other], device
            ).wait_recv()
        block = att_ref[other]
        for i in range(NZ):
            at = lax.div(other, 2) * 8 + i * 2 + lax.rem(other, 2)
            rows = pl.ds(pl.multiple_of(at * 256, 256), 256)
            both = jnp.concatenate(
                [block[i * 32 : i * 32 + 16], block[i * 32 + 16 : i * 32 + 32]], axis=1
            )
            result += jnp.dot(both, w_ref[rows, :], preferred_element_type=F32)
    out_ref[...] = result.astype(BF16)
    for copy in sent:
        copy.wait_send()


def solution(mesh):
    groups, tp = mesh.shape["group"], mesh.shape["tp"]
    nx = tp // 8

    def per_device(queries, new_keys, new_values, key_pages, value_pages, owner, fill, slots, weight):
        tokens = key_pages.shape[1] * PAGE
        width = key_pages.shape[3]
        features, columns = weight.shape
        vmem = pl.BlockSpec(memory_space=pltpu.VMEM)
        hbm = pl.BlockSpec(memory_space=pl.ANY)
        np_ = 2 * nx
        dma = pltpu.SemaphoreType.DMA
        out = pl.pallas_call(
            functools.partial(kernel, groups, nx),
            out_shape=jax.ShapeDtypeStruct((16, columns), BF16),
            in_specs=[hbm] * 9,
            out_specs=vmem,
            scratch_shapes=[
                pltpu.VMEM(queries.shape[1:], BF16),
                pltpu.VMEM(new_keys.shape[1:], BF16),
                pltpu.VMEM(new_values.shape[1:], BF16),
                pltpu.VMEM(owner.shape, jnp.int32),
                pltpu.VMEM(fill.shape, jnp.int32),
                pltpu.SMEM(slots.shape, jnp.int32),
                pltpu.VMEM((tokens, width), BF16),
                pltpu.VMEM((tokens, width), BF16),
                pltpu.VMEM((features, columns), BF16),
                pltpu.VMEM((8, tokens), F32),
                pltpu.VMEM((NZ, 4, 16, HD), BF16),
                pltpu.VMEM((NZ, 2, 16, HD), BF16),
                pltpu.VMEM((NZ, 2, 16, HD), BF16),
                pltpu.VMEM((np_, NZ, 2, 16, HD), BF16),
                pltpu.VMEM((nx, 2, 2, 64, HD), BF16),
                pltpu.VMEM((np_, 2, 64, HD), BF16),
                pltpu.VMEM((HD, HD), F32),
                pltpu.VMEM((np_, 8, HD), F32),
                pltpu.VMEM((np_, 8, HD), F32),
                pltpu.VMEM((NZ, HD, HD), BF16),
                pltpu.VMEM((NZ, 8, HD), F32),
                pltpu.VMEM((16, HD), BF16),
                pltpu.VMEM((8, HD), F32),
                pltpu.VMEM((NZ, 16, HD), BF16),
                pltpu.VMEM((NZ, 8, HD), F32),
                pltpu.VMEM((np_, HD, HD), BF16),
                dma((9,)),
                dma((NZ,)),
                dma((NZ,)),
                dma((NZ,)),
                dma((NZ,)),
                dma,
                dma,
                dma((np_,)),
                dma((np_,)),
                dma((np_,)),
                dma((np_,)),
                dma((np_,)),
                dma((np_,)),
                dma((NZ,)),
                dma((NZ,)),
                dma((NZ,)),
                dma((NZ,)),
                dma((NZ,)),
                dma((NZ,)),
                dma((NZ,)),
                dma((NZ,)),
                dma((np_,)),
                dma((np_,)),
            ],
            compiler_params=pltpu.CompilerParams(
                collective_id=0, has_side_effects=True, vmem_limit_bytes=62 << 20
            ),
        )(
            queries,
            new_keys,
            new_values,
            key_pages[0].reshape(tokens, width),
            value_pages[0].reshape(tokens, width),
            owner,
            fill,
            slots,
            weight,
        )
        return out.reshape(2, 8, columns).transpose(1, 0, 2)[None]

    placed = (
        P("group", None, None, "tp"),
        P("group", None, None, "tp"),
        P("group", None, None, "tp"),
        P("group", "tp", None, None),
        P("group", "tp", None, None),
        P("group", "tp"),
        P("group", "tp"),
        P("group", None),
        P(None, "tp"),
    )
    return jax.shard_map(
        per_device,
        mesh=mesh,
        in_specs=placed,
        out_specs=P("group", None, None, "tp"),
        check_vma=False,
    )
```

```python
import functools
import math

import jax
import jax.numpy as jnp
from jax import lax
from jax.experimental import pallas as pl
from jax.experimental.pallas import tpu as pltpu
from jax.sharding import PartitionSpec as P

HD = 128
PAGE = 16
NZ = 4
NEG = -1e30
C2 = math.log2(math.e) / math.sqrt(HD)
MESH = pl.DeviceIdType.MESH
F32 = jnp.float32
BF16 = jnp.bfloat16


def iota(shape, dim):
    return lax.broadcasted_iota(jnp.int32, shape, dim)


def kernel(
    groups,
    nx,
    q_hbm,
    nk_hbm,
    nv_hbm,
    k_hbm,
    v_hbm,
    owner_hbm,
    fill_hbm,
    slot_hbm,
    w_hbm,
    out_ref,
    q_ref,
    nk_ref,
    nv_ref,
    owner_ref,
    fill_ref,
    slot_ref,
    table_ref,
    other_ref,
    k_ref,
    v_ref,
    w_ref,
    bias_ref,
    score_ref,
    weight_ref,
    line_ref,
    sib_ref,
    qall_ref,
    qout_ref,
    qmov_ref,
    aout_ref,
    arecv_ref,
    mout_ref,
    mrecv_ref,
    sout_ref,
    srecv_ref,
    precv_ref,
    zacc_ref,
    zstat_ref,
    att_ref,
    load_sem,
    line_send,
    line_recv,
    new_send,
    new_recv,
    slot_send,
    slot_recv,
    sib_send,
    sib_recv,
    q_send,
    q_recv,
    qm_send,
    qm_recv,
    a_send,
    a_recv,
    s_send,
    s_recv,
    m_send,
    m_recv,
    p_send,
    p_recv,
    z_send,
    z_recv,
    y_send,
    y_recv,
    o_send,
    o_recv,
):
    np_ = nx * 2
    tokens = k_ref.shape[0]
    pages = owner_ref.shape[1]
    g = lax.axis_index("group")
    t = lax.axis_index("tp")
    x = lax.div(t, 8)
    z = lax.rem(lax.div(t, 2), NZ)
    c = lax.rem(t, 2)
    pp = x * 2 + c
    partner = lax.rem(g + groups // 2, groups)
    sibling = (g, x * 8 + z * 2 + (1 - c))

    def at(group, k, cc):
        xk = lax.rem(x + k, nx)
        return xk * 2 + cc, (group, xk * 8 + z * 2 + cc)

    far = [k for k in (2, 1, 3) if k < nx]
    plane = [(k, cc) for k in far for cc in range(2)] + [(0, 1 - c)]
    near = [(0, 1 - c)] + [(k, cc) for k in (1, 3, 2) if k < nx for cc in range(2)]
    whole = [(k, cc) for k in (0, 1, 3, 2) if k < nx for cc in range(2)]
    line = []
    for other in (3 * (1 - lax.div(z, 2)), lax.rem(2 + 3 * z, 5), 1 + lax.rem(z, 2)):
        line.append((other, (g, x * 8 + other * 2 + c)))

    def remote(src, dst, send, recv, device):
        return pltpu.make_async_remote_copy(
            src_ref=src,
            dst_ref=dst,
            send_sem=send,
            recv_sem=recv,
            device_id=device,
            device_id_type=MESH,
        )

    sent = []

    def send(*args):
        copy = remote(*args)
        copy.start()
        sent.append(copy)

    def arrive(dst, recv):
        remote(dst, dst, slot_send, recv, sibling).wait_recv()

    def fetch(src, dst, at):
        copy = pltpu.make_async_copy(src, dst, load_sem.at[at])
        copy.start()
        return copy

    barrier = pltpu.get_barrier_semaphore()
    greeted = [device for _, device in line]
    greeted.append(at(partner, 0, c)[1])
    greeted += [at(g, k, cc)[1] for k, cc in plane]
    for device in greeted:
        pl.semaphore_signal(barrier, inc=1, device_id=device, device_id_type=MESH)

    first = [fetch(q_hbm.at[0], q_ref, 3), fetch(slot_hbm, table_ref, 9)]
    small = [
        fetch(slot_hbm, slot_ref, 8),
        fetch(nk_hbm.at[0], nk_ref, 4),
        fetch(nv_hbm.at[0], nv_ref, 5),
        fetch(owner_hbm, owner_ref, 6),
        fetch(fill_hbm, fill_ref, 7),
    ]
    loads = [fetch(k_hbm, k_ref, 0), fetch(v_hbm, v_ref, 1), fetch(w_hbm, w_ref, 2)]
    for copy in first:
        copy.wait()

    order = (
        iota((16, 16), 1)
        == 2 * lax.rem(iota((16, 16), 0), 8) + lax.div(iota((16, 16), 0), 8)
    ).astype(BF16)

    def by_step(ref):
        rows = ref[...].reshape(16, ref.shape[2])
        return jnp.dot(order, rows, preferred_element_type=F32).astype(BF16)

    query = by_step(q_ref)
    line_ref[z, 0] = query[:, :HD]
    line_ref[z, 1] = query[:, HD:]

    pl.semaphore_wait(barrier, len(greeted))

    send(table_ref, other_ref, slot_send, slot_recv, at(partner, 0, c)[1])
    for i, (other, device) in enumerate(line):
        send(
            line_ref.at[z, 0:2], line_ref.at[z, 0:2], line_send.at[i], line_recv.at[z], device
        )

    for copy in small:
        copy.wait()
    place = (iota((32, HD), 1) == iota((32, HD), 0) + 32 * lax.rem(t, 4)).astype(BF16)
    line_ref[z, 2] = jnp.dot(by_step(nk_ref), place, preferred_element_type=F32).astype(BF16)
    line_ref[z, 3] = jnp.dot(by_step(nv_ref), place, preferred_element_type=F32).astype(BF16)
    owned = jnp.where(
        jnp.broadcast_to(owner_ref[...], (8, pages)) == iota((8, pages), 0),
        jnp.broadcast_to(fill_ref[...], (8, pages)),
        0,
    )
    spread = (lax.div(iota((pages, tokens), 1), PAGE) == iota((pages, tokens), 0)).astype(BF16)
    held = jnp.dot(owned.astype(F32).astype(BF16), spread, preferred_element_type=F32)
    within = lax.rem(iota((8, tokens), 1), PAGE).astype(F32)
    bias_ref[...] = jnp.where(within < held, 0.0, NEG)

    slots = [slot_ref[0, r] for r in range(8)]
    sub8 = iota((8, HD), 0)
    lane8 = lax.rem(iota((8, HD), 1), 8)
    moving = jnp.zeros((8, HD), jnp.int32)
    moving_lane = jnp.zeros((8, HD), jnp.int32)
    for r in range(8):
        goes = jnp.where(slots[r] < 8, 1, 0)
        moving = jnp.where(sub8 == r, goes, moving)
        moving_lane = jnp.where(lane8 == r, goes, moving_lane)

    def moving_rows(count):
        return jnp.concatenate([moving] * (count // 8), axis=0) == 1

    row = iota((16, HD), 1)
    same = lax.div(row, 8) == iota((16, HD), 0)
    take = (same & (jnp.concatenate([moving_lane, moving_lane], axis=0) == 1)).astype(BF16)

    arrive(other_ref, slot_recv)
    wanted = jnp.where(other_ref[...] < 8, other_ref[...], 0)
    wanted = jnp.max(wanted, axis=1, keepdims=True)
    mover = jnp.where(other_ref[...] < 8, iota((1, 8), 1), 0)
    mover = jnp.max(mover, axis=1, keepdims=True)
    lane16 = lax.rem(iota((2 * np_, HD), 1), 8)
    from_lane = lane16 == jnp.broadcast_to(mover, (2 * np_, HD))
    to_lane = lane16 == jnp.broadcast_to(wanted, (2 * np_, HD))
    fetch_row = (same & (lax.rem(row, 8) == jnp.broadcast_to(wanted, (16, HD)))).astype(BF16)
    for other, _ in line:
        arrive(line_ref.at[other, 0:2], line_recv.at[other])
    lines = [line_ref[i, e] for i in range(NZ) for e in range(2)]
    for i in range(NZ):
        for e in range(2):
            qall_ref[pp, i, e] = lines[2 * i + e]
    qout_ref[...] = jnp.dot(
        fetch_row, jnp.concatenate(lines, axis=0), preferred_element_type=F32
    ).astype(BF16)
    for i, (k, cc) in enumerate(whole):
        send(qout_ref, qmov_ref.at[pp], qm_send.at[i], qm_recv.at[pp], at(partner, k, cc)[1])
    for i, (k, cc) in enumerate(near):
        send(qall_ref.at[pp], qall_ref.at[pp], q_send.at[i], q_recv.at[pp], at(g, k, cc)[1])
    for i, (other, device) in enumerate(line):
        send(line_ref.at[z, 2:4], line_ref.at[z, 2:4], new_send.at[i], new_recv.at[z], device)

    lane = iota((HD, HD), 1)
    loads[0].wait()
    loads[1].wait()

    keep = jnp.where(moving_rows(16), 0.0, 1.0).astype(BF16)
    keep = jnp.concatenate([keep] * 8, axis=0)
    spread8 = (
        (iota((HD, 16), 1) == lax.div(iota((HD, 16), 0), 8)) & moving_rows(HD)[:, 0:16]
    ).astype(BF16)

    def head(k, b):
        return pl.ds(pl.multiple_of((lax.rem(x + k, nx) * 2 + b) * HD, HD), HD)

    def score(k, b):
        xk = lax.rem(x + k, nx)
        query = jnp.concatenate(
            [qall_ref[xk * 2 + cc, 2 * b : 2 * b + 2].reshape(64, HD) for cc in range(2)], axis=0
        )
        moved = jnp.concatenate(
            [qmov_ref[xk * 2 + cc].astype(F32)[8 * b : 8 * b + 8] for cc in range(2)], axis=0
        ).astype(BF16)
        moved = jnp.dot(spread8, moved, preferred_element_type=F32).astype(BF16)
        query = query * keep + moved
        score = lax.dot_general(
            query, k_ref[:, head(k, b)], (((1,), (1,)), ((), ())), preferred_element_type=F32
        )
        score = (score.reshape(16, 8, tokens) + bias_ref[...][None]).reshape(HD, tokens)
        score_ref[k % 2, b] = score
        return jnp.max(score, axis=1, keepdims=True)

    def weigh(k, b, top):
        weight = jnp.exp2((score_ref[k % 2, b] - top) * C2)
        weight_ref[k % 2, b] = weight.astype(BF16)
        return jnp.sum(weight, axis=1, keepdims=True)

    def gather(k, b):
        acc = jnp.dot(weight_ref[k % 2, b], v_ref[:, head(k, b)], preferred_element_type=F32)
        acc = acc.astype(BF16)
        for cc in range(2):
            aout_ref[k, cc, b] = acc[cc * 64 : cc * 64 + 64]
        return jnp.dot(take, acc, preferred_element_type=F32)

    def ready(k):
        for cc in range(2):
            source, _ = at(g, k, cc)
            arrive(qmov_ref.at[source], qm_recv.at[source])
        for cc in range(2) if k else (1 - c,):
            source, _ = at(g, k, cc)
            arrive(qall_ref.at[source], q_recv.at[source])

    def pass_on(k, tops, sums, few):
        stat = jnp.zeros((HD, HD), F32)
        for cc in range(2):
            part = slice(cc * 64, cc * 64 + 64)
            rows = slice(cc * 8, cc * 8 + 8)
            top = jnp.concatenate([tops[0][part], tops[1][part]], axis=0)
            total = jnp.concatenate([sums[0][part], sums[1][part]], axis=0)
            stat = jnp.where(lane == cc * 8, top, jnp.where(lane == cc * 8 + 1, total, stat))
            mout_ref[k, cc] = jnp.concatenate([few[0][rows], few[1][rows]], axis=0).astype(BF16)
        stat = stat.T
        for cc in range(2):
            sout_ref[k, cc] = stat[cc * 8 : cc * 8 + 8]
        for cc in range(2):
            i = k * 2 + cc
            device = at(partner, k, cc)[1]
            send(sout_ref.at[k, cc], precv_ref.at[pp], p_send.at[i], p_recv.at[pp], device)
            send(mout_ref.at[k, cc], mrecv_ref.at[pp], m_send.at[i], m_recv.at[pp], device)
        for cc in range(2) if k else (1 - c,):
            i = k * 2 + cc
            device = at(g, k, cc)[1]
            send(sout_ref.at[k, cc], srecv_ref.at[pp], s_send.at[i], s_recv.at[pp], device)
            send(aout_ref.at[k, cc], arecv_ref.at[pp], a_send.at[i], a_recv.at[pp], device)

    turns = [k for k in (1, 2, 3, 0) if k < nx]
    ready(turns[0])
    tops = [score(turns[0], b) for b in range(2)]
    for k, after in zip(turns, turns[1:] + [None]):
        if after is not None:
            ready(after)
        later, sums = [], []
        for b in range(2):
            if after is not None:
                later.append(score(after, b))
            sums.append(weigh(k, b, tops[b]))
        pass_on(k, tops, sums, [gather(k, b) for b in range(2)])
        tops = later
    for other, _ in line:
        arrive(line_ref.at[other, 2:4], new_recv.at[other])
    send(line_ref.at[:, 2:4], sib_ref, sib_send, sib_recv, sibling)
    arecv_ref[pp] = aout_ref[0, c]
    srecv_ref[pp] = sout_ref[0, c]

    arrive(sib_ref, sib_recv)
    tops, sums, news = [], [], []
    late = lax.rem(iota((8, 8, HD), 0), 2) == 1
    for b in range(2):
        new = [
            sum(
                line_ref[2 * b + i, 2 + kv].astype(F32) + sib_ref[2 * b + i, kv].astype(F32)
                for i in range(2)
            )
            for kv in range(2)
        ]
        query = line_ref[2 * b : 2 * b + 2, 0:2].astype(F32).reshape(8, 8, HD)
        first = jnp.sum(query * new[0][0:8][None], axis=2, keepdims=True)
        second = jnp.sum(query * new[0][8:16][None], axis=2, keepdims=True)
        first = jnp.broadcast_to(first, (8, 8, HD))
        second = jnp.where(late, jnp.broadcast_to(second, (8, 8, HD)), NEG)
        top = jnp.maximum(first, second)
        first = jnp.exp2((first - top) * C2)
        second = jnp.exp2((second - top) * C2)
        tops.append(top.reshape(64, HD))
        sums.append((first + second).reshape(64, HD))
        news.append((first * new[1][0:8][None] + second * new[1][8:16][None]).reshape(64, HD))
    new_acc = jnp.concatenate(news, axis=0)
    new_stat = jnp.where(
        lane == 0,
        jnp.concatenate(tops, axis=0),
        jnp.where(lane == 1, jnp.concatenate(sums, axis=0), 0.0),
    ).T
    new_top, new_sum = new_stat[0:1], new_stat[1:2]

    for k, cc in whole:
        source, _ = at(g, k, cc)
        arrive(precv_ref.at[source], p_recv.at[source])
    came = jnp.concatenate(
        [precv_ref[i, kind : kind + 1] for kind in range(2) for i in range(np_)], axis=0
    )
    came = jnp.where(from_lane, came, NEG)
    for step in (1, 2, 4):
        low = lax.rem(lax.div(lane16, step), 2) == 0
        came = jnp.maximum(
            came, jnp.where(low, pltpu.roll(came, HD - step, 1), pltpu.roll(came, step, 1))
        )
    came = jnp.where(to_lane, came, jnp.where(iota((2 * np_, HD), 0) < np_, NEG, 0.0))
    for k, cc in plane:
        source, _ = at(g, k, cc)
        arrive(srecv_ref.at[source], s_recv.at[source])
    tops = jnp.concatenate([srecv_ref[i, 0:1] for i in range(np_)], axis=0)
    tops = jnp.where(jnp.broadcast_to(moving_lane[0:1] == 1, (np_, HD)), NEG, tops)
    tops = jnp.concatenate([tops, came[:np_]], axis=0)
    sums = [srecv_ref[i, 1:2] for i in range(np_)]
    sums = jnp.concatenate(sums + [came[np_:]], axis=0)
    top8 = jnp.max(tops, axis=0, keepdims=True)
    scale = jnp.exp2((tops - top8) * C2)
    sum8 = jnp.sum(scale * sums, axis=0, keepdims=True)
    zstat_ref[z] = jnp.where(sub8 == 0, top8, jnp.where(sub8 == 1, sum8, 0.0))
    for i, (other, device) in enumerate(line):
        send(zstat_ref.at[z], zstat_ref.at[z], y_send.at[i], y_recv.at[z], device)
    scale = scale.T
    for k, cc in whole:
        source, _ = at(g, k, cc)
        arrive(mrecv_ref.at[source], m_recv.at[source])
    acc = jnp.zeros((16, 8, HD), F32)
    for i in range(np_):
        weight = scale[:, np_ + i : np_ + i + 1].reshape(16, 8, 1)
        acc += weight * mrecv_ref[i].astype(F32)[:, None, :]
    acc = acc.reshape(HD, HD)
    for k, cc in plane:
        source, _ = at(g, k, cc)
        arrive(arecv_ref.at[source], a_recv.at[source])
    for i in range(np_):
        acc += scale[:, i : i + 1] * arecv_ref[i].reshape(HD, HD).astype(F32)
    zacc_ref[z] = acc.astype(BF16)
    for i, (other, device) in enumerate(line):
        send(zacc_ref.at[z], zacc_ref.at[z], z_send.at[i], z_recv.at[z], device)

    for other, _ in line:
        arrive(zstat_ref.at[other], y_recv.at[other])
    tops = jnp.concatenate([zstat_ref[i, 0:1] for i in range(NZ)] + [new_top] * 4, axis=0)
    sums = jnp.concatenate([zstat_ref[i, 1:2] for i in range(NZ)] + [new_sum] * 4, axis=0)
    top = jnp.max(tops, axis=0, keepdims=True)
    scale = jnp.exp2((tops - top) * C2)
    scale = jnp.where((sub8 <= NZ), scale, 0.0)
    scale = (scale / jnp.sum(scale * sums, axis=0, keepdims=True)).T
    acc = scale[:, NZ : NZ + 1] * new_acc
    for other, _ in line:
        arrive(zacc_ref.at[other], z_recv.at[other])
    for i in range(NZ):
        acc += scale[:, i : i + 1] * zacc_ref[i].astype(F32)
    att_ref[pp] = acc.astype(BF16)
    for i, (k, cc) in enumerate(plane):
        send(att_ref.at[pp], att_ref.at[pp], o_send.at[i], o_recv.at[pp], at(g, k, cc)[1])

    loads[2].wait()
    result = jnp.zeros((16, out_ref.shape[1]), F32)
    for k, cc in [(0, c)] + near:
        source, _ = at(g, k, cc)
        if k or cc is not c:
            arrive(att_ref.at[source], o_recv.at[source])
        block = att_ref[source]
        for i in range(NZ):
            head = lax.div(source, 2) * 8 + i * 2 + lax.rem(source, 2)
            rows = pl.ds(pl.multiple_of(head * 256, 256), 256)
            both = jnp.concatenate(
                [block[i * 32 : i * 32 + 16], block[i * 32 + 16 : i * 32 + 32]], axis=1
            )
            result += jnp.dot(both, w_ref[rows, :], preferred_element_type=F32)
    out_ref[...] = result.astype(BF16)
    for copy in sent:
        copy.wait_send()


def solution(mesh):
    groups, tp = mesh.shape["group"], mesh.shape["tp"]
    nx = tp // 8

    def per_device(queries, new_keys, new_values, key_pages, value_pages, owner, fill, slots, weight):
        tokens = key_pages.shape[1] * PAGE
        width = key_pages.shape[3]
        features, columns = weight.shape
        vmem = pl.BlockSpec(memory_space=pltpu.VMEM)
        hbm = pl.BlockSpec(memory_space=pltpu.HBM)
        np_ = 2 * nx
        dma = pltpu.SemaphoreType.DMA
        out = pl.pallas_call(
            functools.partial(kernel, groups, nx),
            out_shape=jax.ShapeDtypeStruct((16, columns), BF16),
            in_specs=[hbm] * 9,
            out_specs=vmem,
            scratch_shapes=[
                pltpu.VMEM(queries.shape[1:], BF16),
                pltpu.VMEM(new_keys.shape[1:], BF16),
                pltpu.VMEM(new_values.shape[1:], BF16),
                pltpu.VMEM(owner.shape, jnp.int32),
                pltpu.VMEM(fill.shape, jnp.int32),
                pltpu.SMEM(slots.shape, jnp.int32),
                pltpu.VMEM(slots.shape, jnp.int32),
                pltpu.VMEM(slots.shape, jnp.int32),
                pltpu.VMEM((tokens, width), BF16),
                pltpu.VMEM((tokens, width), BF16),
                pltpu.VMEM((features, columns), BF16),
                pltpu.VMEM((8, tokens), F32),
                pltpu.VMEM((2, 2, HD, tokens), F32),
                pltpu.VMEM((2, 2, HD, tokens), BF16),
                pltpu.VMEM((NZ, 4, 16, HD), BF16),
                pltpu.VMEM((NZ, 2, 16, HD), BF16),
                pltpu.VMEM((np_, NZ, 2, 16, HD), BF16),
                pltpu.VMEM((16, HD), BF16),
                pltpu.VMEM((np_, 16, HD), BF16),
                pltpu.VMEM((nx, 2, 2, 64, HD), BF16),
                pltpu.VMEM((np_, 2, 64, HD), BF16),
                pltpu.VMEM((nx, 2, 16, HD), BF16),
                pltpu.VMEM((np_, 16, HD), BF16),
                pltpu.VMEM((nx, 2, 8, HD), F32),
                pltpu.VMEM((np_, 8, HD), F32),
                pltpu.VMEM((np_, 8, HD), F32),
                pltpu.VMEM((NZ, HD, HD), BF16),
                pltpu.VMEM((NZ, 8, HD), F32),
                pltpu.VMEM((np_, HD, HD), BF16),
                dma((10,)),
                dma((3,)),
                dma((NZ,)),
                dma((3,)),
                dma((NZ,)),
                dma,
                dma,
                dma,
                dma,
            ]
            + [dma((np_,))] * 12
            + [dma((3,)), dma((NZ,))] * 2
            + [dma((np_,))] * 2,
            compiler_params=pltpu.CompilerParams(
                collective_id=0, has_side_effects=True, vmem_limit_bytes=40 << 20
            ),
        )(
            *[
                pltpu.with_memory_space_constraint(a, pltpu.HBM)
                for a in (
                    queries,
                    new_keys,
                    new_values,
                    key_pages[0].reshape(tokens, width),
                    value_pages[0].reshape(tokens, width),
                    owner,
                    fill,
                    slots,
                    weight,
                )
            ]
        )
        return out.reshape(2, 8, columns).transpose(1, 0, 2)[None]

    placed = (
        P("group", None, None, "tp"),
        P("group", None, None, "tp"),
        P("group", None, None, "tp"),
        P("group", "tp", None, None),
        P("group", "tp", None, None),
        P("group", "tp"),
        P("group", "tp"),
        P("group", None),
        P(None, "tp"),
    )
    return jax.shard_map(
        per_device,
        mesh=mesh,
        in_specs=placed,
        out_specs=P("group", None, None, "tp"),
        check_vma=False,
    )
```

```python
import functools
import math

import jax
import jax.numpy as jnp
from jax import lax
from jax.experimental import pallas as pl
from jax.experimental.pallas import tpu as pltpu
from jax.sharding import PartitionSpec as P

HD = 128
PAGE = 16
NZ = 4
NEG = -1e30
C2 = math.log2(math.e) / math.sqrt(HD)
MESH = pl.DeviceIdType.MESH
F32 = jnp.float32
BF16 = jnp.bfloat16


def iota(shape, dim):
    return lax.broadcasted_iota(jnp.int32, shape, dim)


def kernel(
    groups,
    nx,
    q_hbm,
    nk_hbm,
    nv_hbm,
    k_hbm,
    v_hbm,
    owner_hbm,
    fill_hbm,
    slot_hbm,
    w_hbm,
    out_ref,
    q_ref,
    nk_ref,
    nv_ref,
    owner_ref,
    fill_ref,
    slot_ref,
    table_ref,
    other_ref,
    k_ref,
    v_ref,
    w_ref,
    bias_ref,
    score_ref,
    weight_ref,
    line_ref,
    fresh_ref,
    sib_ref,
    qall_ref,
    qout_ref,
    qmov_ref,
    aout_ref,
    arecv_ref,
    mout_ref,
    mrecv_ref,
    sout_ref,
    srecv_ref,
    precv_ref,
    zacc_ref,
    zstat_ref,
    att_ref,
    load_sem,
    line_send,
    line_recv,
    new_send,
    new_recv,
    slot_send,
    slot_recv,
    sib_send,
    sib_recv,
    q_send,
    q_recv,
    qm_send,
    qm_recv,
    a_send,
    a_recv,
    s_send,
    s_recv,
    m_send,
    m_recv,
    p_send,
    p_recv,
    z_send,
    z_recv,
    y_send,
    y_recv,
    o_send,
    o_recv,
):
    np_ = nx * 2
    tokens = k_ref.shape[0]
    pages = owner_ref.shape[1]
    g = lax.axis_index("group")
    t = lax.axis_index("tp")
    x = lax.div(t, 8)
    z = lax.rem(lax.div(t, 2), NZ)
    c = lax.rem(t, 2)
    pp = x * 2 + c
    partner = lax.rem(g + groups // 2, groups)
    sibling = (g, x * 8 + z * 2 + (1 - c))

    def at(group, k, cc):
        xk = lax.rem(x + k, nx)
        return xk * 2 + cc, (group, xk * 8 + z * 2 + cc)

    far = [k for k in (2, 1, 3) if k < nx]
    plane = [(k, cc) for k in far for cc in range(2)] + [(0, 1 - c)]
    near = [(0, 1 - c)] + [(k, cc) for k in (1, 3, 2) if k < nx for cc in range(2)]
    whole = [(k, cc) for k in (0, 1, 3, 2) if k < nx for cc in range(2)]
    line = []
    for other in (3 * (1 - lax.div(z, 2)), lax.rem(2 + 3 * z, 5), 1 + lax.rem(z, 2)):
        line.append((other, (g, x * 8 + other * 2 + c)))

    def remote(src, dst, send, recv, device):
        return pltpu.make_async_remote_copy(
            src_ref=src,
            dst_ref=dst,
            send_sem=send,
            recv_sem=recv,
            device_id=device,
            device_id_type=MESH,
        )

    def send(*args):
        remote(*args).start()

    def left(ref, sem):
        remote(ref, ref, sem, slot_recv, sibling).wait_send()

    def arrive(dst, recv):
        remote(dst, dst, slot_send, recv, sibling).wait_recv()

    def fetch(src, dst, at):
        copy = pltpu.make_async_copy(src, dst, load_sem.at[at])
        copy.start()
        return copy

    barrier = pltpu.get_barrier_semaphore()
    greeted = [device for _, device in line]
    greeted.append(at(partner, 0, c)[1])
    greeted += [at(g, k, cc)[1] for k, cc in plane]
    for device in greeted:
        pl.semaphore_signal(barrier, inc=1, device_id=device, device_id_type=MESH)

    first = [fetch(q_hbm.at[0], q_ref, 3), fetch(slot_hbm, table_ref, 9)]
    small = [
        fetch(slot_hbm, slot_ref, 8),
        fetch(nk_hbm.at[0], nk_ref, 4),
        fetch(nv_hbm.at[0], nv_ref, 5),
        fetch(owner_hbm, owner_ref, 6),
        fetch(fill_hbm, fill_ref, 7),
    ]
    loads = [fetch(k_hbm, k_ref, 0), fetch(v_hbm, v_ref, 1), fetch(w_hbm, w_ref, 2)]
    for copy in first:
        copy.wait()

    order = (
        iota((16, 16), 1)
        == 2 * lax.rem(iota((16, 16), 0), 8) + lax.div(iota((16, 16), 0), 8)
    ).astype(BF16)

    def by_step(ref):
        rows = ref[...].reshape(16, ref.shape[2])
        return jnp.dot(order, rows, preferred_element_type=F32).astype(BF16)

    query = by_step(q_ref)
    line_ref[z, 0] = query[:, :HD]
    line_ref[z, 1] = query[:, HD:]

    pl.semaphore_wait(barrier, len(greeted))

    send(table_ref, other_ref, slot_send, slot_recv, at(partner, 0, c)[1])
    for _, device in line:
        send(
            line_ref.at[z], line_ref.at[z], line_send, line_recv, device
        )

    for copy in small:
        copy.wait()
    place = (iota((32, HD), 1) == iota((32, HD), 0) + 32 * lax.rem(t, 4)).astype(BF16)
    fresh_ref[z, 0] = jnp.dot(by_step(nk_ref), place, preferred_element_type=F32).astype(BF16)
    fresh_ref[z, 1] = jnp.dot(by_step(nv_ref), place, preferred_element_type=F32).astype(BF16)
    owned = jnp.where(
        jnp.broadcast_to(owner_ref[...], (8, pages)) == iota((8, pages), 0),
        jnp.broadcast_to(fill_ref[...], (8, pages)),
        0,
    )
    spread = (lax.div(iota((pages, tokens), 1), PAGE) == iota((pages, tokens), 0)).astype(BF16)
    held = jnp.dot(owned.astype(F32).astype(BF16), spread, preferred_element_type=F32)
    within = lax.rem(iota((8, tokens), 1), PAGE).astype(F32)
    bias_ref[...] = jnp.where(within < held, 0.0, NEG)

    slots = [slot_ref[0, r] for r in range(8)]
    sub8 = iota((8, HD), 0)
    lane8 = lax.rem(iota((8, HD), 1), 8)
    moving = jnp.zeros((8, HD), jnp.int32)
    moving_lane = jnp.zeros((8, HD), jnp.int32)
    for r in range(8):
        goes = jnp.where(slots[r] < 8, 1, 0)
        moving = jnp.where(sub8 == r, goes, moving)
        moving_lane = jnp.where(lane8 == r, goes, moving_lane)

    def moving_rows(count):
        return jnp.concatenate([moving] * (count // 8), axis=0) == 1

    row = iota((16, HD), 1)
    same = lax.div(row, 8) == iota((16, HD), 0)
    take = (same & (jnp.concatenate([moving_lane, moving_lane], axis=0) == 1)).astype(BF16)

    arrive(other_ref, slot_recv)
    wanted = jnp.where(other_ref[...] < 8, other_ref[...], 0)
    wanted = jnp.max(wanted, axis=1, keepdims=True)
    mover = jnp.where(other_ref[...] < 8, iota((1, 8), 1), 0)
    mover = jnp.max(mover, axis=1, keepdims=True)
    lane16 = lax.rem(iota((2 * np_, HD), 1), 8)
    from_lane = lane16 == jnp.broadcast_to(mover, (2 * np_, HD))
    to_lane = lane16 == jnp.broadcast_to(wanted, (2 * np_, HD))
    fetch_row = (same & (lax.rem(row, 8) == jnp.broadcast_to(wanted, (16, HD)))).astype(BF16)
    arrive(line_ref.at[0:3], line_recv)
    lines = [line_ref[i, e] for i in range(NZ) for e in range(2)]
    for i in range(NZ):
        for e in range(2):
            qall_ref[pp, i, e] = lines[2 * i + e]
    qout_ref[...] = jnp.dot(
        fetch_row, jnp.concatenate(lines, axis=0), preferred_element_type=F32
    ).astype(BF16)
    for k, cc in whole:
        turn = (nx - k) % nx
        send(qout_ref, qmov_ref.at[pp], qm_send, qm_recv.at[turn], at(partner, k, cc)[1])
    for k, cc in near:
        turn = (nx - k) % nx
        send(qall_ref.at[pp], qall_ref.at[pp], q_send, q_recv.at[turn], at(g, k, cc)[1])
    for _, device in line:
        send(fresh_ref.at[z], fresh_ref.at[z], new_send, new_recv, device)

    lane = iota((HD, HD), 1)
    loads[0].wait()
    loads[1].wait()

    keep = jnp.where(moving_rows(16), 0.0, 1.0).astype(BF16)
    keep = jnp.concatenate([keep] * 8, axis=0)
    spread8 = (
        (iota((HD, 16), 1) == lax.div(iota((HD, 16), 0), 8)) & moving_rows(HD)[:, 0:16]
    ).astype(BF16)

    def head(k, b):
        return pl.ds(pl.multiple_of((lax.rem(x + k, nx) * 2 + b) * HD, HD), HD)

    def score(k, b):
        xk = lax.rem(x + k, nx)
        query = jnp.concatenate(
            [qall_ref[xk * 2 + cc, 2 * b : 2 * b + 2].reshape(64, HD) for cc in range(2)], axis=0
        )
        moved = jnp.concatenate(
            [qmov_ref[xk * 2 + cc].astype(F32)[8 * b : 8 * b + 8] for cc in range(2)], axis=0
        ).astype(BF16)
        moved = jnp.dot(spread8, moved, preferred_element_type=F32).astype(BF16)
        query = query * keep + moved
        score = lax.dot_general(
            query, k_ref[:, head(k, b)], (((1,), (1,)), ((), ())), preferred_element_type=F32
        )
        score = (score.reshape(16, 8, tokens) + bias_ref[...][None]).reshape(HD, tokens)
        score_ref[k % 2, b] = score
        return jnp.max(score, axis=1, keepdims=True)

    def weigh(k, b, top):
        weight = jnp.exp2((score_ref[k % 2, b] - top) * C2)
        weight_ref[k % 2, b] = weight.astype(BF16)
        return jnp.sum(weight, axis=1, keepdims=True)

    def gather(k, b):
        acc = jnp.dot(weight_ref[k % 2, b], v_ref[:, head(k, b)], preferred_element_type=F32)
        acc = acc.astype(BF16)
        for cc in range(2):
            aout_ref[k, cc, b] = acc[cc * 64 : cc * 64 + 64]
        return jnp.dot(take, acc, preferred_element_type=F32)

    def chip(ref, k, count=2):
        return ref.at[pl.ds(lax.rem(x + k, nx) * 2, count)]

    def ready(k):
        arrive(chip(qmov_ref, k), qm_recv.at[k])
        arrive(chip(qall_ref, k, 2 if k else 1), q_recv.at[k])

    def pass_on(k, tops, sums, few):
        stat = jnp.zeros((HD, HD), F32)
        for cc in range(2):
            part = slice(cc * 64, cc * 64 + 64)
            rows = slice(cc * 8, cc * 8 + 8)
            top = jnp.concatenate([tops[0][part], tops[1][part]], axis=0)
            total = jnp.concatenate([sums[0][part], sums[1][part]], axis=0)
            stat = jnp.where(lane == cc * 8, top, jnp.where(lane == cc * 8 + 1, total, stat))
            mout_ref[k, cc] = jnp.concatenate([few[0][rows], few[1][rows]], axis=0).astype(BF16)
        stat = stat.T
        for cc in range(2):
            sout_ref[k, cc] = stat[cc * 8 : cc * 8 + 8]
        for cc in range(2):
            device = at(partner, k, cc)[1]
            send(sout_ref.at[k, cc], precv_ref.at[pp], p_send, p_recv, device)
            send(mout_ref.at[k, cc], mrecv_ref.at[pp], m_send, m_recv, device)
        for cc in range(2) if k else (1 - c,):
            device = at(g, k, cc)[1]
            send(sout_ref.at[k, cc], srecv_ref.at[pp], s_send, s_recv, device)
            send(aout_ref.at[k, cc], arecv_ref.at[pp], a_send, a_recv, device)

    turns = [k for k in (1, 2, 3, 0) if k < nx]
    ready(turns[0])
    tops = [score(turns[0], b) for b in range(2)]
    for k, after in zip(turns, turns[1:] + [None]):
        if after is not None:
            ready(after)
        later, sums = [], []
        for b in range(2):
            if after is not None:
                later.append(score(after, b))
            sums.append(weigh(k, b, tops[b]))
        pass_on(k, tops, sums, [gather(k, b) for b in range(2)])
        tops = later
    arrive(fresh_ref.at[0:3], new_recv)
    send(fresh_ref, sib_ref, sib_send, sib_recv, sibling)
    arecv_ref[pp] = aout_ref[0, c]
    srecv_ref[pp] = sout_ref[0, c]

    arrive(sib_ref, sib_recv)
    tops, sums, news = [], [], []
    late = lax.rem(iota((8, 8, HD), 0), 2) == 1
    for b in range(2):
        new = [
            sum(
                fresh_ref[2 * b + i, kv].astype(F32) + sib_ref[2 * b + i, kv].astype(F32)
                for i in range(2)
            )
            for kv in range(2)
        ]
        query = line_ref[2 * b : 2 * b + 2].astype(F32).reshape(8, 8, HD)
        first = jnp.sum(query * new[0][0:8][None], axis=2, keepdims=True)
        second = jnp.sum(query * new[0][8:16][None], axis=2, keepdims=True)
        first = jnp.broadcast_to(first, (8, 8, HD))
        second = jnp.where(late, jnp.broadcast_to(second, (8, 8, HD)), NEG)
        top = jnp.maximum(first, second)
        first = jnp.exp2((first - top) * C2)
        second = jnp.exp2((second - top) * C2)
        tops.append(top.reshape(64, HD))
        sums.append((first + second).reshape(64, HD))
        news.append((first * new[1][0:8][None] + second * new[1][8:16][None]).reshape(64, HD))
    new_acc = jnp.concatenate(news, axis=0)
    new_stat = jnp.where(
        lane == 0,
        jnp.concatenate(tops, axis=0),
        jnp.where(lane == 1, jnp.concatenate(sums, axis=0), 0.0),
    ).T
    new_top, new_sum = new_stat[0:1], new_stat[1:2]

    arrive(precv_ref, p_recv)
    came = jnp.concatenate(
        [precv_ref[i, kind : kind + 1] for kind in range(2) for i in range(np_)], axis=0
    )
    came = jnp.where(from_lane, came, NEG)
    for step in (1, 2, 4):
        low = lax.rem(lax.div(lane16, step), 2) == 0
        came = jnp.maximum(
            came, jnp.where(low, pltpu.roll(came, HD - step, 1), pltpu.roll(came, step, 1))
        )
    came = jnp.where(to_lane, came, jnp.where(iota((2 * np_, HD), 0) < np_, NEG, 0.0))
    arrive(srecv_ref.at[0 : np_ - 1], s_recv)
    tops = jnp.concatenate([srecv_ref[i, 0:1] for i in range(np_)], axis=0)
    tops = jnp.where(jnp.broadcast_to(moving_lane[0:1] == 1, (np_, HD)), NEG, tops)
    tops = jnp.concatenate([tops, came[:np_]], axis=0)
    sums = [srecv_ref[i, 1:2] for i in range(np_)]
    sums = jnp.concatenate(sums + [came[np_:]], axis=0)
    top8 = jnp.max(tops, axis=0, keepdims=True)
    scale = jnp.exp2((tops - top8) * C2)
    sum8 = jnp.sum(scale * sums, axis=0, keepdims=True)
    zstat_ref[z] = jnp.where(sub8 == 0, top8, jnp.where(sub8 == 1, sum8, 0.0))
    for _, device in line:
        send(zstat_ref.at[z], zstat_ref.at[z], y_send, y_recv, device)
    scale = scale.T
    arrive(mrecv_ref, m_recv)
    acc = jnp.zeros((16, 8, HD), F32)
    for i in range(np_):
        weight = scale[:, np_ + i : np_ + i + 1].reshape(16, 8, 1)
        acc += weight * mrecv_ref[i].astype(F32)[:, None, :]
    acc = acc.reshape(HD, HD)
    arrive(arecv_ref.at[0 : np_ - 1], a_recv)
    for i in range(np_):
        acc += scale[:, i : i + 1] * arecv_ref[i].reshape(HD, HD).astype(F32)
    zacc_ref[z] = acc.astype(BF16)
    for _, device in line:
        send(zacc_ref.at[z], zacc_ref.at[z], z_send, z_recv, device)

    arrive(zstat_ref.at[0:3], y_recv)
    tops = jnp.concatenate([zstat_ref[i, 0:1] for i in range(NZ)] + [new_top] * 4, axis=0)
    sums = jnp.concatenate([zstat_ref[i, 1:2] for i in range(NZ)] + [new_sum] * 4, axis=0)
    top = jnp.max(tops, axis=0, keepdims=True)
    scale = jnp.exp2((tops - top) * C2)
    scale = jnp.where((sub8 <= NZ), scale, 0.0)
    scale = (scale / jnp.sum(scale * sums, axis=0, keepdims=True)).T
    acc = scale[:, NZ : NZ + 1] * new_acc
    arrive(zacc_ref.at[0:3], z_recv)
    for i in range(NZ):
        acc += scale[:, i : i + 1] * zacc_ref[i].astype(F32)
    att_ref[pp] = acc.astype(BF16)
    for k, cc in plane:
        turn = (nx - k) % nx
        send(att_ref.at[pp], att_ref.at[pp], o_send, o_recv.at[turn], at(g, k, cc)[1])

    loads[2].wait()
    result = jnp.zeros((16, out_ref.shape[1]), F32)
    for k, cc in [(0, c)] + near:
        source, _ = at(g, k, cc)
        if k and cc == 0:
            arrive(chip(att_ref, k), o_recv.at[k])
        elif k == 0 and cc is not c:
            arrive(att_ref.at[source], o_recv.at[k])
        block = att_ref[source]
        for i in range(NZ):
            head = lax.div(source, 2) * 8 + i * 2 + lax.rem(source, 2)
            rows = pl.ds(pl.multiple_of(head * 256, 256), 256)
            both = jnp.concatenate(
                [block[i * 32 : i * 32 + 16], block[i * 32 + 16 : i * 32 + 32]], axis=1
            )
            result += jnp.dot(both, w_ref[rows, :], preferred_element_type=F32)
    out_ref[...] = result.astype(BF16)
    left(table_ref, slot_send)
    left(line_ref.at[0:3], line_send)
    left(fresh_ref.at[0:3], new_send)
    left(fresh_ref, sib_send)
    left(qall_ref.at[0 : np_ - 1], q_send)
    left(qmov_ref, qm_send)
    left(arecv_ref.at[0 : np_ - 1], a_send)
    left(srecv_ref.at[0 : np_ - 1], s_send)
    left(mrecv_ref, m_send)
    left(precv_ref, p_send)
    left(zacc_ref.at[0:3], z_send)
    left(zstat_ref.at[0:3], y_send)
    left(att_ref.at[0 : np_ - 1], o_send)


def solution(mesh):
    groups, tp = mesh.shape["group"], mesh.shape["tp"]
    nx = tp // 8

    def per_device(queries, new_keys, new_values, key_pages, value_pages, owner, fill, slots, weight):
        tokens = key_pages.shape[1] * PAGE
        width = key_pages.shape[3]
        features, columns = weight.shape
        vmem = pl.BlockSpec(memory_space=pltpu.VMEM)
        hbm = pl.BlockSpec(memory_space=pltpu.HBM)
        np_ = 2 * nx
        dma = pltpu.SemaphoreType.DMA
        out = pl.pallas_call(
            functools.partial(kernel, groups, nx),
            out_shape=jax.ShapeDtypeStruct((16, columns), BF16),
            in_specs=[hbm] * 9,
            out_specs=vmem,
            scratch_shapes=[
                pltpu.VMEM(queries.shape[1:], BF16),
                pltpu.VMEM(new_keys.shape[1:], BF16),
                pltpu.VMEM(new_values.shape[1:], BF16),
                pltpu.VMEM(owner.shape, jnp.int32),
                pltpu.VMEM(fill.shape, jnp.int32),
                pltpu.SMEM(slots.shape, jnp.int32),
                pltpu.VMEM(slots.shape, jnp.int32),
                pltpu.VMEM(slots.shape, jnp.int32),
                pltpu.VMEM((tokens, width), BF16),
                pltpu.VMEM((tokens, width), BF16),
                pltpu.VMEM((features, columns), BF16),
                pltpu.VMEM((8, tokens), F32),
                pltpu.VMEM((2, 2, HD, tokens), F32),
                pltpu.VMEM((2, 2, HD, tokens), BF16),
                pltpu.VMEM((NZ, 2, 16, HD), BF16),
                pltpu.VMEM((NZ, 2, 16, HD), BF16),
                pltpu.VMEM((NZ, 2, 16, HD), BF16),
                pltpu.VMEM((np_, NZ, 2, 16, HD), BF16),
                pltpu.VMEM((16, HD), BF16),
                pltpu.VMEM((np_, 16, HD), BF16),
                pltpu.VMEM((nx, 2, 2, 64, HD), BF16),
                pltpu.VMEM((np_, 2, 64, HD), BF16),
                pltpu.VMEM((nx, 2, 16, HD), BF16),
                pltpu.VMEM((np_, 16, HD), BF16),
                pltpu.VMEM((nx, 2, 8, HD), F32),
                pltpu.VMEM((np_, 8, HD), F32),
                pltpu.VMEM((np_, 8, HD), F32),
                pltpu.VMEM((NZ, HD, HD), BF16),
                pltpu.VMEM((NZ, 8, HD), F32),
                pltpu.VMEM((np_, HD, HD), BF16),
                dma((10,)),
            ]
            + [dma] * 8
            + [dma, dma((nx,))] * 2
            + [dma] * 12
            + [dma, dma((nx,))],
            compiler_params=pltpu.CompilerParams(
                collective_id=0, has_side_effects=True, vmem_limit_bytes=40 << 20
            ),
        )(
            *[
                pltpu.with_memory_space_constraint(a, pltpu.HBM)
                for a in (
                    queries,
                    new_keys,
                    new_values,
                    key_pages[0].reshape(tokens, width),
                    value_pages[0].reshape(tokens, width),
                    owner,
                    fill,
                    slots,
                    weight,
                )
            ]
        )
        return out.reshape(2, 8, columns).transpose(1, 0, 2)[None]

    placed = (
        P("group", None, None, "tp"),
        P("group", None, None, "tp"),
        P("group", None, None, "tp"),
        P("group", "tp", None, None),
        P("group", "tp", None, None),
        P("group", "tp"),
        P("group", "tp"),
        P("group", None),
        P(None, "tp"),
    )
    return jax.shard_map(
        per_device,
        mesh=mesh,
        in_specs=placed,
        out_specs=P("group", None, None, "tp"),
        check_vma=False,
    )
```

```python
import functools
import math

import jax
import jax.numpy as jnp
from jax import lax
from jax.experimental import pallas as pl
from jax.experimental.pallas import tpu as pltpu
from jax.sharding import PartitionSpec as P

HD = 128
PAGE = 16
NZ = 4
NEG = -1e30
C2 = math.log2(math.e) / math.sqrt(HD)
MESH = pl.DeviceIdType.MESH
F32 = jnp.float32
BF16 = jnp.bfloat16


def iota(shape, dim):
    return lax.broadcasted_iota(jnp.int32, shape, dim)


def kernel(
    groups,
    nx,
    q_hbm,
    nk_hbm,
    nv_hbm,
    k_hbm,
    v_hbm,
    owner_hbm,
    fill_hbm,
    slot_hbm,
    w_hbm,
    out_ref,
    q_ref,
    nk_ref,
    nv_ref,
    owner_ref,
    fill_ref,
    slot_ref,
    table_ref,
    other_ref,
    k_ref,
    v_ref,
    w_ref,
    bias_ref,
    score_ref,
    weight_ref,
    line_ref,
    fresh_ref,
    sib_ref,
    qall_ref,
    qout_ref,
    qmov_ref,
    aout_ref,
    arecv_ref,
    mout_ref,
    mrecv_ref,
    sout_ref,
    srecv_ref,
    precv_ref,
    zacc_ref,
    zstat_ref,
    att_ref,
    load_sem,
    line_send,
    line_recv,
    new_send,
    new_recv,
    slot_send,
    slot_recv,
    sib_send,
    sib_recv,
    q_send,
    q_recv,
    qm_send,
    qm_recv,
    a_send,
    a_recv,
    s_send,
    s_recv,
    m_send,
    m_recv,
    p_send,
    p_recv,
    z_send,
    z_recv,
    y_send,
    y_recv,
    o_send,
    o_recv,
):
    np_ = nx * 2
    tokens = k_ref.shape[0]
    pages = owner_ref.shape[1]
    g = lax.axis_index("group")
    t = lax.axis_index("tp")
    x = lax.div(t, 8)
    z = lax.rem(lax.div(t, 2), NZ)
    c = lax.rem(t, 2)
    pp = x * 2 + c
    partner = lax.rem(g + groups // 2, groups)
    sibling = (g, x * 8 + z * 2 + (1 - c))

    def at(group, k, cc):
        xk = lax.rem(x + k, nx)
        return xk * 2 + cc, (group, xk * 8 + z * 2 + cc)

    far = [k for k in (2, 1, 3) if k < nx]
    plane = [(k, cc) for k in far for cc in range(2)] + [(0, 1 - c)]
    near = [(0, 1 - c)] + [(k, cc) for k in (1, 3, 2) if k < nx for cc in range(2)]
    whole = [(k, cc) for k in (0, 1, 3, 2) if k < nx for cc in range(2)]
    line = []
    for other in (3 * (1 - lax.div(z, 2)), lax.rem(2 + 3 * z, 5), 1 + lax.rem(z, 2)):
        line.append((other, (g, x * 8 + other * 2 + c)))

    def remote(src, dst, send, recv, device):
        return pltpu.make_async_remote_copy(
            src_ref=src,
            dst_ref=dst,
            send_sem=send,
            recv_sem=recv,
            device_id=device,
            device_id_type=MESH,
        )

    def send(*args):
        remote(*args).start()

    def left(ref, sem):
        remote(ref, ref, sem, slot_recv, sibling).wait_send()

    def arrive(dst, recv):
        remote(dst, dst, slot_send, recv, sibling).wait_recv()

    def fetch(src, dst, at):
        copy = pltpu.make_async_copy(src, dst, load_sem.at[at])
        copy.start()
        return copy

    barrier = pltpu.get_barrier_semaphore()
    greeted = [device for _, device in line]
    greeted.append(at(partner, 0, c)[1])
    greeted += [at(g, k, cc)[1] for k, cc in plane]
    for device in greeted:
        pl.semaphore_signal(barrier, inc=1, device_id=device, device_id_type=MESH)

    first = [fetch(q_hbm.at[0], q_ref, 3), fetch(slot_hbm, table_ref, 9)]
    small = [
        fetch(slot_hbm, slot_ref, 8),
        fetch(nk_hbm.at[0], nk_ref, 4),
        fetch(nv_hbm.at[0], nv_ref, 5),
        fetch(owner_hbm, owner_ref, 6),
        fetch(fill_hbm, fill_ref, 7),
    ]
    loads = [fetch(k_hbm, k_ref, 0), fetch(v_hbm, v_ref, 1), fetch(w_hbm, w_ref, 2)]
    for copy in first:
        copy.wait()

    order = (
        iota((16, 16), 1)
        == 2 * lax.rem(iota((16, 16), 0), 8) + lax.div(iota((16, 16), 0), 8)
    ).astype(BF16)

    def by_step(ref):
        rows = ref[...].reshape(16, ref.shape[2])
        return jnp.dot(order, rows, preferred_element_type=F32).astype(BF16)

    query = by_step(q_ref)
    line_ref[z, 0] = query[:, :HD]
    line_ref[z, 1] = query[:, HD:]

    pl.semaphore_wait(barrier, len(greeted))

    send(table_ref, other_ref, slot_send, slot_recv, at(partner, 0, c)[1])
    for _, device in line:
        send(
            line_ref.at[z], line_ref.at[z], line_send, line_recv.at[z], device
        )

    def relay(other):
        qall_ref[pp, other] = line_ref[other]
        for k, cc in near:
            turn = (nx - k) % nx
            send(
                line_ref.at[other],
                qall_ref.at[pp, other],
                q_send,
                q_recv.at[turn],
                at(g, k, cc)[1],
            )

    relay(z)

    for copy in small:
        copy.wait()
    place = (iota((32, HD), 1) == iota((32, HD), 0) + 32 * lax.rem(t, 4)).astype(BF16)
    fresh_ref[z, 0] = jnp.dot(by_step(nk_ref), place, preferred_element_type=F32).astype(BF16)
    fresh_ref[z, 1] = jnp.dot(by_step(nv_ref), place, preferred_element_type=F32).astype(BF16)
    owned = jnp.where(
        jnp.broadcast_to(owner_ref[...], (8, pages)) == iota((8, pages), 0),
        jnp.broadcast_to(fill_ref[...], (8, pages)),
        0,
    )
    spread = (lax.div(iota((pages, tokens), 1), PAGE) == iota((pages, tokens), 0)).astype(BF16)
    held = jnp.dot(owned.astype(F32).astype(BF16), spread, preferred_element_type=F32)
    within = lax.rem(iota((8, tokens), 1), PAGE).astype(F32)
    bias_ref[...] = jnp.where(within < held, 0.0, NEG)

    slots = [slot_ref[0, r] for r in range(8)]
    sub8 = iota((8, HD), 0)
    lane8 = lax.rem(iota((8, HD), 1), 8)
    moving = jnp.zeros((8, HD), jnp.int32)
    moving_lane = jnp.zeros((8, HD), jnp.int32)
    for r in range(8):
        goes = jnp.where(slots[r] < 8, 1, 0)
        moving = jnp.where(sub8 == r, goes, moving)
        moving_lane = jnp.where(lane8 == r, goes, moving_lane)

    def moving_rows(count):
        return jnp.concatenate([moving] * (count // 8), axis=0) == 1

    row = iota((16, HD), 1)
    same = lax.div(row, 8) == iota((16, HD), 0)
    take = (same & (jnp.concatenate([moving_lane, moving_lane], axis=0) == 1)).astype(BF16)

    for other, _ in line[:0:-1]:
        arrive(line_ref.at[other], line_recv.at[other])
        relay(other)
    arrive(other_ref, slot_recv)
    wanted = jnp.where(other_ref[...] < 8, other_ref[...], 0)
    wanted = jnp.max(wanted, axis=1, keepdims=True)
    mover = jnp.where(other_ref[...] < 8, iota((1, 8), 1), 0)
    mover = jnp.max(mover, axis=1, keepdims=True)
    lane16 = lax.rem(iota((2 * np_, HD), 1), 8)
    from_lane = lane16 == jnp.broadcast_to(mover, (2 * np_, HD))
    to_lane = lane16 == jnp.broadcast_to(wanted, (2 * np_, HD))
    fetch_row = (same & (lax.rem(row, 8) == jnp.broadcast_to(wanted, (16, HD)))).astype(BF16)
    last = line[0][0]
    arrive(line_ref.at[last], line_recv.at[last])
    lines = [line_ref[i, e] for i in range(NZ) for e in range(2)]
    qout_ref[...] = jnp.dot(
        fetch_row, jnp.concatenate(lines, axis=0), preferred_element_type=F32
    ).astype(BF16)
    for k, cc in whole:
        turn = (nx - k) % nx
        send(qout_ref, qmov_ref.at[pp], qm_send, qm_recv.at[turn], at(partner, k, cc)[1])
    relay(last)
    for _, device in line:
        send(fresh_ref.at[z], fresh_ref.at[z], new_send, new_recv, device)

    lane = iota((HD, HD), 1)
    loads[0].wait()
    loads[1].wait()

    keep = jnp.where(moving_rows(16), 0.0, 1.0).astype(BF16)
    keep = jnp.concatenate([keep] * 8, axis=0)
    spread8 = (
        (iota((HD, 16), 1) == lax.div(iota((HD, 16), 0), 8)) & moving_rows(HD)[:, 0:16]
    ).astype(BF16)

    def head(k, b):
        return pl.ds(pl.multiple_of((lax.rem(x + k, nx) * 2 + b) * HD, HD), HD)

    def score(k, b):
        xk = lax.rem(x + k, nx)
        query = jnp.concatenate(
            [qall_ref[xk * 2 + cc, 2 * b : 2 * b + 2].reshape(64, HD) for cc in range(2)], axis=0
        )
        moved = jnp.concatenate(
            [qmov_ref[xk * 2 + cc].astype(F32)[8 * b : 8 * b + 8] for cc in range(2)], axis=0
        ).astype(BF16)
        moved = jnp.dot(spread8, moved, preferred_element_type=F32).astype(BF16)
        query = query * keep + moved
        score = lax.dot_general(
            query, k_ref[:, head(k, b)], (((1,), (1,)), ((), ())), preferred_element_type=F32
        )
        score = (score.reshape(16, 8, tokens) + bias_ref[...][None]).reshape(HD, tokens)
        score_ref[k % 2, b] = score
        return jnp.max(score, axis=1, keepdims=True)

    def weigh(k, b, top):
        weight = jnp.exp2((score_ref[k % 2, b] - top) * C2)
        weight_ref[k % 2, b] = weight.astype(BF16)
        return jnp.sum(weight, axis=1, keepdims=True)

    def gather(k, b):
        acc = jnp.dot(weight_ref[k % 2, b], v_ref[:, head(k, b)], preferred_element_type=F32)
        acc = acc.astype(BF16)
        for cc in range(2):
            aout_ref[k, cc, b] = acc[cc * 64 : cc * 64 + 64]
        return jnp.dot(take, acc, preferred_element_type=F32)

    def chip(ref, k, count=2):
        return ref.at[pl.ds(lax.rem(x + k, nx) * 2, count)]

    def ready(k):
        arrive(chip(qmov_ref, k), qm_recv.at[k])
        arrive(chip(qall_ref, k, 2 if k else 1), q_recv.at[k])

    def pass_on(k, tops, sums, few):
        stat = jnp.zeros((HD, HD), F32)
        for cc in range(2):
            part = slice(cc * 64, cc * 64 + 64)
            rows = slice(cc * 8, cc * 8 + 8)
            top = jnp.concatenate([tops[0][part], tops[1][part]], axis=0)
            total = jnp.concatenate([sums[0][part], sums[1][part]], axis=0)
            stat = jnp.where(lane == cc * 8, top, jnp.where(lane == cc * 8 + 1, total, stat))
            mout_ref[k, cc] = jnp.concatenate([few[0][rows], few[1][rows]], axis=0).astype(BF16)
        stat = stat.T
        for cc in range(2):
            sout_ref[k, cc] = stat[cc * 8 : cc * 8 + 8]
        for cc in range(2):
            device = at(partner, k, cc)[1]
            send(sout_ref.at[k, cc], precv_ref.at[pp], p_send, p_recv, device)
            send(mout_ref.at[k, cc], mrecv_ref.at[pp], m_send, m_recv, device)
        for cc in range(2) if k else (1 - c,):
            device = at(g, k, cc)[1]
            send(sout_ref.at[k, cc], srecv_ref.at[pp], s_send, s_recv, device)
            send(aout_ref.at[k, cc], arecv_ref.at[pp], a_send, a_recv, device)

    turns = [k for k in (1, 2, 3, 0) if k < nx]
    ready(turns[0])
    tops = [score(turns[0], b) for b in range(2)]
    for k, after in zip(turns, turns[1:] + [None]):
        if after is not None:
            ready(after)
        later, sums = [], []
        for b in range(2):
            if after is not None:
                later.append(score(after, b))
            sums.append(weigh(k, b, tops[b]))
        pass_on(k, tops, sums, [gather(k, b) for b in range(2)])
        tops = later
    arrive(fresh_ref.at[0:3], new_recv)
    send(fresh_ref, sib_ref, sib_send, sib_recv, sibling)
    arecv_ref[pp] = aout_ref[0, c]
    srecv_ref[pp] = sout_ref[0, c]

    arrive(sib_ref, sib_recv)
    tops, sums, news = [], [], []
    late = lax.rem(iota((8, 8, HD), 0), 2) == 1
    for b in range(2):
        new = [
            sum(
                fresh_ref[2 * b + i, kv].astype(F32) + sib_ref[2 * b + i, kv].astype(F32)
                for i in range(2)
            )
            for kv in range(2)
        ]
        query = line_ref[2 * b : 2 * b + 2].astype(F32).reshape(8, 8, HD)
        first = jnp.sum(query * new[0][0:8][None], axis=2, keepdims=True)
        second = jnp.sum(query * new[0][8:16][None], axis=2, keepdims=True)
        first = jnp.broadcast_to(first, (8, 8, HD))
        second = jnp.where(late, jnp.broadcast_to(second, (8, 8, HD)), NEG)
        top = jnp.maximum(first, second)
        first = jnp.exp2((first - top) * C2)
        second = jnp.exp2((second - top) * C2)
        tops.append(top.reshape(64, HD))
        sums.append((first + second).reshape(64, HD))
        news.append((first * new[1][0:8][None] + second * new[1][8:16][None]).reshape(64, HD))
    new_acc = jnp.concatenate(news, axis=0)
    new_stat = jnp.where(
        lane == 0,
        jnp.concatenate(tops, axis=0),
        jnp.where(lane == 1, jnp.concatenate(sums, axis=0), 0.0),
    ).T
    new_top, new_sum = new_stat[0:1], new_stat[1:2]

    arrive(precv_ref, p_recv)
    came = jnp.concatenate(
        [precv_ref[i, kind : kind + 1] for kind in range(2) for i in range(np_)], axis=0
    )
    came = jnp.where(from_lane, came, NEG)
    for step in (1, 2, 4):
        low = lax.rem(lax.div(lane16, step), 2) == 0
        came = jnp.maximum(
            came, jnp.where(low, pltpu.roll(came, HD - step, 1), pltpu.roll(came, step, 1))
        )
    came = jnp.where(to_lane, came, jnp.where(iota((2 * np_, HD), 0) < np_, NEG, 0.0))
    arrive(srecv_ref.at[0 : np_ - 1], s_recv)
    tops = jnp.concatenate([srecv_ref[i, 0:1] for i in range(np_)], axis=0)
    tops = jnp.where(jnp.broadcast_to(moving_lane[0:1] == 1, (np_, HD)), NEG, tops)
    tops = jnp.concatenate([tops, came[:np_]], axis=0)
    sums = [srecv_ref[i, 1:2] for i in range(np_)]
    sums = jnp.concatenate(sums + [came[np_:]], axis=0)
    top8 = jnp.max(tops, axis=0, keepdims=True)
    scale = jnp.exp2((tops - top8) * C2)
    sum8 = jnp.sum(scale * sums, axis=0, keepdims=True)
    zstat_ref[z] = jnp.where(sub8 == 0, top8, jnp.where(sub8 == 1, sum8, 0.0))
    for _, device in line:
        send(zstat_ref.at[z], zstat_ref.at[z], y_send, y_recv, device)
    scale = scale.T
    arrive(mrecv_ref, m_recv)
    acc = jnp.zeros((16, 8, HD), F32)
    for i in range(np_):
        weight = scale[:, np_ + i : np_ + i + 1].reshape(16, 8, 1)
        acc += weight * mrecv_ref[i].astype(F32)[:, None, :]
    acc = acc.reshape(HD, HD)
    arrive(arecv_ref.at[0 : np_ - 1], a_recv)
    for i in range(np_):
        acc += scale[:, i : i + 1] * arecv_ref[i].reshape(HD, HD).astype(F32)
    zacc_ref[z] = acc.astype(BF16)
    for _, device in line:
        send(zacc_ref.at[z], zacc_ref.at[z], z_send, z_recv, device)

    arrive(zstat_ref.at[0:3], y_recv)
    tops = jnp.concatenate([zstat_ref[i, 0:1] for i in range(NZ)] + [new_top] * 4, axis=0)
    sums = jnp.concatenate([zstat_ref[i, 1:2] for i in range(NZ)] + [new_sum] * 4, axis=0)
    top = jnp.max(tops, axis=0, keepdims=True)
    scale = jnp.exp2((tops - top) * C2)
    scale = jnp.where((sub8 <= NZ), scale, 0.0)
    scale = (scale / jnp.sum(scale * sums, axis=0, keepdims=True)).T
    acc = scale[:, NZ : NZ + 1] * new_acc
    arrive(zacc_ref.at[0:3], z_recv)
    for i in range(NZ):
        acc += scale[:, i : i + 1] * zacc_ref[i].astype(F32)
    att_ref[pp] = acc.astype(BF16)
    for k, cc in plane:
        turn = (nx - k) % nx
        send(att_ref.at[pp], att_ref.at[pp], o_send, o_recv.at[turn], at(g, k, cc)[1])

    loads[2].wait()
    result = jnp.zeros((16, out_ref.shape[1]), F32)
    for k, cc in [(0, c)] + near:
        source, _ = at(g, k, cc)
        if k and cc == 0:
            arrive(chip(att_ref, k), o_recv.at[k])
        elif k == 0 and cc is not c:
            arrive(att_ref.at[source], o_recv.at[k])
        block = att_ref[source]
        for i in range(NZ):
            head = lax.div(source, 2) * 8 + i * 2 + lax.rem(source, 2)
            rows = pl.ds(pl.multiple_of(head * 256, 256), 256)
            both = jnp.concatenate(
                [block[i * 32 : i * 32 + 16], block[i * 32 + 16 : i * 32 + 32]], axis=1
            )
            result += jnp.dot(both, w_ref[rows, :], preferred_element_type=F32)
    out_ref[...] = result.astype(BF16)
    left(table_ref, slot_send)
    left(line_ref.at[0:3], line_send)
    left(fresh_ref.at[0:3], new_send)
    left(fresh_ref, sib_send)
    left(qall_ref.at[0 : np_ - 1], q_send)
    left(qmov_ref, qm_send)
    left(arecv_ref.at[0 : np_ - 1], a_send)
    left(srecv_ref.at[0 : np_ - 1], s_send)
    left(mrecv_ref, m_send)
    left(precv_ref, p_send)
    left(zacc_ref.at[0:3], z_send)
    left(zstat_ref.at[0:3], y_send)
    left(att_ref.at[0 : np_ - 1], o_send)


def solution(mesh):
    groups, tp = mesh.shape["group"], mesh.shape["tp"]
    nx = tp // 8

    def per_device(queries, new_keys, new_values, key_pages, value_pages, owner, fill, slots, weight):
        tokens = key_pages.shape[1] * PAGE
        width = key_pages.shape[3]
        features, columns = weight.shape
        vmem = pl.BlockSpec(memory_space=pltpu.VMEM)
        hbm = pl.BlockSpec(memory_space=pltpu.HBM)
        np_ = 2 * nx
        dma = pltpu.SemaphoreType.DMA
        out = pl.pallas_call(
            functools.partial(kernel, groups, nx),
            out_shape=jax.ShapeDtypeStruct((16, columns), BF16),
            in_specs=[hbm] * 9,
            out_specs=vmem,
            scratch_shapes=[
                pltpu.VMEM(queries.shape[1:], BF16),
                pltpu.VMEM(new_keys.shape[1:], BF16),
                pltpu.VMEM(new_values.shape[1:], BF16),
                pltpu.VMEM(owner.shape, jnp.int32),
                pltpu.VMEM(fill.shape, jnp.int32),
                pltpu.SMEM(slots.shape, jnp.int32),
                pltpu.VMEM(slots.shape, jnp.int32),
                pltpu.VMEM(slots.shape, jnp.int32),
                pltpu.VMEM((tokens, width), BF16),
                pltpu.VMEM((tokens, width), BF16),
                pltpu.VMEM((features, columns), BF16),
                pltpu.VMEM((8, tokens), F32),
                pltpu.VMEM((2, 2, HD, tokens), F32),
                pltpu.VMEM((2, 2, HD, tokens), BF16),
                pltpu.VMEM((NZ, 2, 16, HD), BF16),
                pltpu.VMEM((NZ, 2, 16, HD), BF16),
                pltpu.VMEM((NZ, 2, 16, HD), BF16),
                pltpu.VMEM((np_, NZ, 2, 16, HD), BF16),
                pltpu.VMEM((16, HD), BF16),
                pltpu.VMEM((np_, 16, HD), BF16),
                pltpu.VMEM((nx, 2, 2, 64, HD), BF16),
                pltpu.VMEM((np_, 2, 64, HD), BF16),
                pltpu.VMEM((nx, 2, 16, HD), BF16),
                pltpu.VMEM((np_, 16, HD), BF16),
                pltpu.VMEM((nx, 2, 8, HD), F32),
                pltpu.VMEM((np_, 8, HD), F32),
                pltpu.VMEM((np_, 8, HD), F32),
                pltpu.VMEM((NZ, HD, HD), BF16),
                pltpu.VMEM((NZ, 8, HD), F32),
                pltpu.VMEM((np_, HD, HD), BF16),
                dma((10,)),
            ]
            + [dma, dma((NZ,))]
            + [dma] * 6
            + [dma, dma((nx,))] * 2
            + [dma] * 12
            + [dma, dma((nx,))],
            compiler_params=pltpu.CompilerParams(
                collective_id=0, has_side_effects=True, vmem_limit_bytes=40 << 20
            ),
        )(
            *[
                pltpu.with_memory_space_constraint(a, pltpu.HBM)
                for a in (
                    queries,
                    new_keys,
                    new_values,
                    key_pages[0].reshape(tokens, width),
                    value_pages[0].reshape(tokens, width),
                    owner,
                    fill,
                    slots,
                    weight,
                )
            ]
        )
        return out.reshape(2, 8, columns).transpose(1, 0, 2)[None]

    placed = (
        P("group", None, None, "tp"),
        P("group", None, None, "tp"),
        P("group", None, None, "tp"),
        P("group", "tp", None, None),
        P("group", "tp", None, None),
        P("group", "tp"),
        P("group", "tp"),
        P("group", None),
        P(None, "tp"),
    )
    return jax.shard_map(
        per_device,
        mesh=mesh,
        in_specs=placed,
        out_specs=P("group", None, None, "tp"),
        check_vma=False,
    )
```

```python
import functools
import math

import jax
import jax.numpy as jnp
from jax import lax
from jax.experimental import pallas as pl
from jax.experimental.pallas import tpu as pltpu
from jax.sharding import PartitionSpec as P

HD = 128
PAGE = 16
NZ = 4
NEG = -1e30
C2 = math.log2(math.e) / math.sqrt(HD)
MESH = pl.DeviceIdType.MESH
F32 = jnp.float32
BF16 = jnp.bfloat16


def iota(shape, dim):
    return lax.broadcasted_iota(jnp.int32, shape, dim)


def kernel(
    groups,
    nx,
    q_hbm,
    nk_hbm,
    nv_hbm,
    k_hbm,
    v_hbm,
    owner_hbm,
    fill_hbm,
    slot_hbm,
    w_hbm,
    out_ref,
    q_ref,
    nk_ref,
    nv_ref,
    owner_ref,
    fill_ref,
    slot_ref,
    table_ref,
    other_ref,
    k_ref,
    v_ref,
    w_ref,
    bias_ref,
    score_ref,
    weight_ref,
    line_ref,
    fresh_ref,
    sib_ref,
    qall_ref,
    qout_ref,
    qmov_ref,
    aout_ref,
    arecv_ref,
    mout_ref,
    mrecv_ref,
    sout_ref,
    srecv_ref,
    precv_ref,
    zacc_ref,
    zstat_ref,
    att_ref,
    load_sem,
    all_send,
    line_recv,
    new_recv,
    slot_send,
    slot_recv,
    sib_recv,
    q_recv,
    qm_recv,
    a_recv,
    s_recv,
    m_recv,
    p_recv,
    z_recv,
    y_recv,
    o_recv,
):
    np_ = nx * 2
    tokens = k_ref.shape[0]
    pages = owner_ref.shape[1]
    g = lax.axis_index("group")
    t = lax.axis_index("tp")
    x = lax.div(t, 8)
    z = lax.rem(lax.div(t, 2), NZ)
    c = lax.rem(t, 2)
    pp = x * 2 + c
    partner = lax.rem(g + groups // 2, groups)
    sibling = (g, x * 8 + z * 2 + (1 - c))

    def at(group, k, cc):
        xk = lax.rem(x + k, nx)
        return xk * 2 + cc, (group, xk * 8 + z * 2 + cc)

    far = [k for k in (2, 1, 3) if k < nx]
    plane = [(k, cc) for k in far for cc in range(2)] + [(0, 1 - c)]
    near = [(0, 1 - c)] + [(k, cc) for k in (1, 3, 2) if k < nx for cc in range(2)]
    whole = [(k, cc) for k in (0, 1, 3, 2) if k < nx for cc in range(2)]
    line = []
    for other in (3 * (1 - lax.div(z, 2)), lax.rem(2 + 3 * z, 5), 1 + lax.rem(z, 2)):
        line.append((other, (g, x * 8 + other * 2 + c)))

    def remote(src, dst, send, recv, device):
        return pltpu.make_async_remote_copy(
            src_ref=src,
            dst_ref=dst,
            send_sem=send,
            recv_sem=recv,
            device_id=device,
            device_id_type=MESH,
        )

    def send(*args):
        remote(*args).start()

    def left(ref, sem):
        remote(ref, ref, sem, slot_recv, sibling).wait_send()

    def arrive(dst, recv):
        remote(dst, dst, slot_send, recv, sibling).wait_recv()

    def fetch(src, dst, at):
        copy = pltpu.make_async_copy(src, dst, load_sem.at[at])
        copy.start()
        return copy

    barrier = pltpu.get_barrier_semaphore()
    greeted = [device for _, device in line]
    greeted.append(at(partner, 0, c)[1])
    greeted += [at(g, k, cc)[1] for k, cc in plane]
    for device in greeted:
        pl.semaphore_signal(barrier, inc=1, device_id=device, device_id_type=MESH)

    first = [fetch(q_hbm.at[0], q_ref, 3), fetch(slot_hbm, table_ref, 9)]
    small = [
        fetch(slot_hbm, slot_ref, 8),
        fetch(nk_hbm.at[0], nk_ref, 4),
        fetch(nv_hbm.at[0], nv_ref, 5),
        fetch(owner_hbm, owner_ref, 6),
        fetch(fill_hbm, fill_ref, 7),
    ]
    loads = [fetch(k_hbm, k_ref, 0), fetch(v_hbm, v_ref, 1), fetch(w_hbm, w_ref, 2)]
    for copy in first:
        copy.wait()

    order = (
        iota((16, 16), 1)
        == 2 * lax.rem(iota((16, 16), 0), 8) + lax.div(iota((16, 16), 0), 8)
    ).astype(BF16)

    def by_step(ref):
        rows = ref[...].reshape(16, ref.shape[2])
        return jnp.dot(order, rows, preferred_element_type=F32).astype(BF16)

    query = by_step(q_ref)
    line_ref[z, 0] = query[:, :HD]
    line_ref[z, 1] = query[:, HD:]

    pl.semaphore_wait(barrier, len(greeted))

    send(table_ref, other_ref, slot_send, slot_recv, at(partner, 0, c)[1])
    for _, device in line:
        send(
            line_ref.at[z], line_ref.at[z], all_send, line_recv, device
        )

    for copy in small:
        copy.wait()
    place = (iota((32, HD), 1) == iota((32, HD), 0) + 32 * lax.rem(t, 4)).astype(BF16)
    fresh_ref[z, 0] = jnp.dot(by_step(nk_ref), place, preferred_element_type=F32).astype(BF16)
    fresh_ref[z, 1] = jnp.dot(by_step(nv_ref), place, preferred_element_type=F32).astype(BF16)
    owned = jnp.where(
        jnp.broadcast_to(owner_ref[...], (8, pages)) == iota((8, pages), 0),
        jnp.broadcast_to(fill_ref[...], (8, pages)),
        0,
    )
    spread = (lax.div(iota((pages, tokens), 1), PAGE) == iota((pages, tokens), 0)).astype(BF16)
    held = jnp.dot(owned.astype(F32).astype(BF16), spread, preferred_element_type=F32)
    within = lax.rem(iota((8, tokens), 1), PAGE).astype(F32)
    bias_ref[...] = jnp.where(within < held, 0.0, NEG)

    slots = [slot_ref[0, r] for r in range(8)]
    sub8 = iota((8, HD), 0)
    lane8 = lax.rem(iota((8, HD), 1), 8)
    moving = jnp.zeros((8, HD), jnp.int32)
    moving_lane = jnp.zeros((8, HD), jnp.int32)
    for r in range(8):
        goes = jnp.where(slots[r] < 8, 1, 0)
        moving = jnp.where(sub8 == r, goes, moving)
        moving_lane = jnp.where(lane8 == r, goes, moving_lane)

    def moving_rows(count):
        return jnp.concatenate([moving] * (count // 8), axis=0) == 1

    row = iota((16, HD), 1)
    same = lax.div(row, 8) == iota((16, HD), 0)
    take = (same & (jnp.concatenate([moving_lane, moving_lane], axis=0) == 1)).astype(BF16)

    arrive(other_ref, slot_recv)
    wanted = jnp.where(other_ref[...] < 8, other_ref[...], 0)
    wanted = jnp.max(wanted, axis=1, keepdims=True)
    mover = jnp.where(other_ref[...] < 8, iota((1, 8), 1), 0)
    mover = jnp.max(mover, axis=1, keepdims=True)
    lane16 = lax.rem(iota((2 * np_, HD), 1), 8)
    from_lane = lane16 == jnp.broadcast_to(mover, (2 * np_, HD))
    to_lane = lane16 == jnp.broadcast_to(wanted, (2 * np_, HD))
    fetch_row = (same & (lax.rem(row, 8) == jnp.broadcast_to(wanted, (16, HD)))).astype(BF16)
    arrive(line_ref.at[0:3], line_recv)
    lines = [line_ref[i, e] for i in range(NZ) for e in range(2)]
    for i in range(NZ):
        for e in range(2):
            qall_ref[pp, i, e] = lines[2 * i + e]
    qout_ref[...] = jnp.dot(
        fetch_row, jnp.concatenate(lines, axis=0), preferred_element_type=F32
    ).astype(BF16)
    for k, cc in whole:
        turn = (nx - k) % nx
        send(qout_ref, qmov_ref.at[pp], all_send, qm_recv.at[turn], at(partner, k, cc)[1])
    for k, cc in near:
        turn = (nx - k) % nx
        send(qall_ref.at[pp], qall_ref.at[pp], all_send, q_recv.at[turn], at(g, k, cc)[1])
    for _, device in line:
        send(fresh_ref.at[z], fresh_ref.at[z], all_send, new_recv, device)

    lane = iota((HD, HD), 1)
    loads[0].wait()
    loads[1].wait()

    keep = jnp.where(moving_rows(16), 0.0, 1.0).astype(BF16)
    keep = jnp.concatenate([keep] * 8, axis=0)
    spread8 = (
        (iota((HD, 16), 1) == lax.div(iota((HD, 16), 0), 8)) & moving_rows(HD)[:, 0:16]
    ).astype(BF16)

    def head(k, b):
        return pl.ds(pl.multiple_of((lax.rem(x + k, nx) * 2 + b) * HD, HD), HD)

    def score(k, b):
        xk = lax.rem(x + k, nx)
        query = jnp.concatenate(
            [qall_ref[xk * 2 + cc, 2 * b : 2 * b + 2].reshape(64, HD) for cc in range(2)], axis=0
        )
        moved = jnp.concatenate(
            [qmov_ref[xk * 2 + cc].astype(F32)[8 * b : 8 * b + 8] for cc in range(2)], axis=0
        ).astype(BF16)
        moved = jnp.dot(spread8, moved, preferred_element_type=F32).astype(BF16)
        query = query * keep + moved
        score = lax.dot_general(
            query, k_ref[:, head(k, b)], (((1,), (1,)), ((), ())), preferred_element_type=F32
        )
        score = (score.reshape(16, 8, tokens) + bias_ref[...][None]).reshape(HD, tokens)
        score_ref[k % 2, b] = score
        return jnp.max(score, axis=1, keepdims=True)

    def weigh(k, b, top):
        weight = jnp.exp2((score_ref[k % 2, b] - top) * C2)
        weight_ref[k % 2, b] = weight.astype(BF16)
        return jnp.sum(weight, axis=1, keepdims=True)

    def gather(k, b):
        acc = jnp.dot(weight_ref[k % 2, b], v_ref[:, head(k, b)], preferred_element_type=F32)
        acc = acc.astype(BF16)
        for cc in range(2):
            aout_ref[k, cc, b] = acc[cc * 64 : cc * 64 + 64]
        return jnp.dot(take, acc, preferred_element_type=F32)

    def chip(ref, k, count=2):
        return ref.at[pl.ds(lax.rem(x + k, nx) * 2, count)]

    def ready(k):
        arrive(chip(qmov_ref, k), qm_recv.at[k])
        arrive(chip(qall_ref, k, 2 if k else 1), q_recv.at[k])

    def pass_on(k, tops, sums, few):
        stat = jnp.zeros((HD, HD), F32)
        for cc in range(2):
            part = slice(cc * 64, cc * 64 + 64)
            rows = slice(cc * 8, cc * 8 + 8)
            top = jnp.concatenate([tops[0][part], tops[1][part]], axis=0)
            total = jnp.concatenate([sums[0][part], sums[1][part]], axis=0)
            stat = jnp.where(lane == cc * 8, top, jnp.where(lane == cc * 8 + 1, total, stat))
            mout_ref[k, cc] = jnp.concatenate([few[0][rows], few[1][rows]], axis=0).astype(BF16)
        stat = stat.T
        for cc in range(2):
            sout_ref[k, cc] = stat[cc * 8 : cc * 8 + 8]
        for cc in range(2):
            device = at(partner, k, cc)[1]
            send(sout_ref.at[k, cc], precv_ref.at[pp], all_send, p_recv, device)
            send(mout_ref.at[k, cc], mrecv_ref.at[pp], all_send, m_recv, device)
        for cc in range(2) if k else (1 - c,):
            device = at(g, k, cc)[1]
            send(sout_ref.at[k, cc], srecv_ref.at[pp], all_send, s_recv, device)
            send(aout_ref.at[k, cc], arecv_ref.at[pp], all_send, a_recv, device)

    turns = [k for k in (1, 2, 3, 0) if k < nx]
    ready(turns[0])
    tops = [score(turns[0], b) for b in range(2)]
    for k, after in zip(turns, turns[1:] + [None]):
        if after is not None:
            ready(after)
        later, sums = [], []
        for b in range(2):
            if after is not None:
                later.append(score(after, b))
            sums.append(weigh(k, b, tops[b]))
        pass_on(k, tops, sums, [gather(k, b) for b in range(2)])
        tops = later
    arrive(fresh_ref.at[0:3], new_recv)
    send(fresh_ref, sib_ref, all_send, sib_recv, sibling)
    arecv_ref[pp] = aout_ref[0, c]
    srecv_ref[pp] = sout_ref[0, c]

    arrive(sib_ref, sib_recv)
    tops, sums, news = [], [], []
    late = lax.rem(iota((8, 8, HD), 0), 2) == 1
    for b in range(2):
        new = [
            sum(
                fresh_ref[2 * b + i, kv].astype(F32) + sib_ref[2 * b + i, kv].astype(F32)
                for i in range(2)
            )
            for kv in range(2)
        ]
        query = line_ref[2 * b : 2 * b + 2].astype(F32).reshape(8, 8, HD)
        first = jnp.sum(query * new[0][0:8][None], axis=2, keepdims=True)
        second = jnp.sum(query * new[0][8:16][None], axis=2, keepdims=True)
        first = jnp.broadcast_to(first, (8, 8, HD))
        second = jnp.where(late, jnp.broadcast_to(second, (8, 8, HD)), NEG)
        top = jnp.maximum(first, second)
        first = jnp.exp2((first - top) * C2)
        second = jnp.exp2((second - top) * C2)
        tops.append(top.reshape(64, HD))
        sums.append((first + second).reshape(64, HD))
        news.append((first * new[1][0:8][None] + second * new[1][8:16][None]).reshape(64, HD))
    new_acc = jnp.concatenate(news, axis=0)
    new_stat = jnp.where(
        lane == 0,
        jnp.concatenate(tops, axis=0),
        jnp.where(lane == 1, jnp.concatenate(sums, axis=0), 0.0),
    ).T
    new_top, new_sum = new_stat[0:1], new_stat[1:2]

    arrive(precv_ref, p_recv)
    came = jnp.concatenate(
        [precv_ref[i, kind : kind + 1] for kind in range(2) for i in range(np_)], axis=0
    )
    came = jnp.where(from_lane, came, NEG)
    for step in (1, 2, 4):
        low = lax.rem(lax.div(lane16, step), 2) == 0
        came = jnp.maximum(
            came, jnp.where(low, pltpu.roll(came, HD - step, 1), pltpu.roll(came, step, 1))
        )
    came = jnp.where(to_lane, came, jnp.where(iota((2 * np_, HD), 0) < np_, NEG, 0.0))
    arrive(srecv_ref.at[0 : np_ - 1], s_recv)
    tops = jnp.concatenate([srecv_ref[i, 0:1] for i in range(np_)], axis=0)
    tops = jnp.where(jnp.broadcast_to(moving_lane[0:1] == 1, (np_, HD)), NEG, tops)
    tops = jnp.concatenate([tops, came[:np_]], axis=0)
    sums = [srecv_ref[i, 1:2] for i in range(np_)]
    sums = jnp.concatenate(sums + [came[np_:]], axis=0)
    top8 = jnp.max(tops, axis=0, keepdims=True)
    scale = jnp.exp2((tops - top8) * C2)
    sum8 = jnp.sum(scale * sums, axis=0, keepdims=True)
    zstat_ref[z] = jnp.where(sub8 == 0, top8, jnp.where(sub8 == 1, sum8, 0.0))
    for _, device in line:
        send(zstat_ref.at[z], zstat_ref.at[z], all_send, y_recv, device)
    scale = scale.T
    arrive(mrecv_ref, m_recv)
    acc = jnp.zeros((16, 8, HD), F32)
    for i in range(np_):
        weight = scale[:, np_ + i : np_ + i + 1].reshape(16, 8, 1)
        acc += weight * mrecv_ref[i].astype(F32)[:, None, :]
    acc = acc.reshape(HD, HD)
    arrive(arecv_ref.at[0 : np_ - 1], a_recv)
    for i in range(np_):
        acc += scale[:, i : i + 1] * arecv_ref[i].reshape(HD, HD).astype(F32)
    zacc_ref[z] = acc.astype(BF16)
    for _, device in line:
        send(zacc_ref.at[z], zacc_ref.at[z], all_send, z_recv, device)

    arrive(zstat_ref.at[0:3], y_recv)
    tops = jnp.concatenate([zstat_ref[i, 0:1] for i in range(NZ)] + [new_top] * 4, axis=0)
    sums = jnp.concatenate([zstat_ref[i, 1:2] for i in range(NZ)] + [new_sum] * 4, axis=0)
    top = jnp.max(tops, axis=0, keepdims=True)
    scale = jnp.exp2((tops - top) * C2)
    scale = jnp.where((sub8 <= NZ), scale, 0.0)
    scale = (scale / jnp.sum(scale * sums, axis=0, keepdims=True)).T
    acc = scale[:, NZ : NZ + 1] * new_acc
    arrive(zacc_ref.at[0:3], z_recv)
    for i in range(NZ):
        acc += scale[:, i : i + 1] * zacc_ref[i].astype(F32)
    att_ref[pp] = acc.astype(BF16)
    for k, cc in plane:
        turn = (nx - k) % nx
        send(att_ref.at[pp], att_ref.at[pp], all_send, o_recv.at[turn], at(g, k, cc)[1])

    loads[2].wait()
    result = jnp.zeros((16, out_ref.shape[1]), F32)
    for k, cc in [(0, c)] + near:
        source, _ = at(g, k, cc)
        if k and cc == 0:
            arrive(chip(att_ref, k), o_recv.at[k])
        elif k == 0 and cc is not c:
            arrive(att_ref.at[source], o_recv.at[k])
        block = att_ref[source]
        for i in range(NZ):
            head = lax.div(source, 2) * 8 + i * 2 + lax.rem(source, 2)
            rows = pl.ds(pl.multiple_of(head * 256, 256), 256)
            both = jnp.concatenate(
                [block[i * 32 : i * 32 + 16], block[i * 32 + 16 : i * 32 + 32]], axis=1
            )
            result += jnp.dot(both, w_ref[rows, :], preferred_element_type=F32)
    out_ref[...] = result.astype(BF16)
    left(table_ref, slot_send)
    blocks = 8 * (3 * (np_ - 1) + 3 + 1) + 2 * 6 + 3 * np_ + (np_ - 1) + 3
    left(w_ref.at[0 : blocks * 16 * HD // w_ref.shape[1]], all_send)


def solution(mesh):
    groups, tp = mesh.shape["group"], mesh.shape["tp"]
    nx = tp // 8

    def per_device(queries, new_keys, new_values, key_pages, value_pages, owner, fill, slots, weight):
        tokens = key_pages.shape[1] * PAGE
        width = key_pages.shape[3]
        features, columns = weight.shape
        vmem = pl.BlockSpec(memory_space=pltpu.VMEM)
        hbm = pl.BlockSpec(memory_space=pltpu.HBM)
        np_ = 2 * nx
        dma = pltpu.SemaphoreType.DMA
        out = pl.pallas_call(
            functools.partial(kernel, groups, nx),
            out_shape=jax.ShapeDtypeStruct((16, columns), BF16),
            in_specs=[hbm] * 9,
            out_specs=vmem,
            scratch_shapes=[
                pltpu.VMEM(queries.shape[1:], BF16),
                pltpu.VMEM(new_keys.shape[1:], BF16),
                pltpu.VMEM(new_values.shape[1:], BF16),
                pltpu.VMEM(owner.shape, jnp.int32),
                pltpu.VMEM(fill.shape, jnp.int32),
                pltpu.SMEM(slots.shape, jnp.int32),
                pltpu.VMEM(slots.shape, jnp.int32),
                pltpu.VMEM(slots.shape, jnp.int32),
                pltpu.VMEM((tokens, width), BF16),
                pltpu.VMEM((tokens, width), BF16),
                pltpu.VMEM((features, columns), BF16),
                pltpu.VMEM((8, tokens), F32),
                pltpu.VMEM((2, 2, HD, tokens), F32),
                pltpu.VMEM((2, 2, HD, tokens), BF16),
                pltpu.VMEM((NZ, 2, 16, HD), BF16),
                pltpu.VMEM((NZ, 2, 16, HD), BF16),
                pltpu.VMEM((NZ, 2, 16, HD), BF16),
                pltpu.VMEM((np_, NZ, 2, 16, HD), BF16),
                pltpu.VMEM((16, HD), BF16),
                pltpu.VMEM((np_, 16, HD), BF16),
                pltpu.VMEM((nx, 2, 2, 64, HD), BF16),
                pltpu.VMEM((np_, 2, 64, HD), BF16),
                pltpu.VMEM((nx, 2, 16, HD), BF16),
                pltpu.VMEM((np_, 16, HD), BF16),
                pltpu.VMEM((nx, 2, 8, HD), F32),
                pltpu.VMEM((np_, 8, HD), F32),
                pltpu.VMEM((np_, 8, HD), F32),
                pltpu.VMEM((NZ, HD, HD), BF16),
                pltpu.VMEM((NZ, 8, HD), F32),
                pltpu.VMEM((np_, HD, HD), BF16),
                dma((10,)),
            ]
            + [dma] * 6
            + [dma((nx,))] * 2
            + [dma] * 6
            + [dma((nx,))],
            compiler_params=pltpu.CompilerParams(
                collective_id=0, has_side_effects=True, vmem_limit_bytes=40 << 20
            ),
        )(
            *[
                pltpu.with_memory_space_constraint(a, pltpu.HBM)
                for a in (
                    queries,
                    new_keys,
                    new_values,
                    key_pages[0].reshape(tokens, width),
                    value_pages[0].reshape(tokens, width),
                    owner,
                    fill,
                    slots,
                    weight,
                )
            ]
        )
        return out.reshape(2, 8, columns).transpose(1, 0, 2)[None]

    placed = (
        P("group", None, None, "tp"),
        P("group", None, None, "tp"),
        P("group", None, None, "tp"),
        P("group", "tp", None, None),
        P("group", "tp", None, None),
        P("group", "tp"),
        P("group", "tp"),
        P("group", None),
        P(None, "tp"),
    )
    return jax.shard_map(
        per_device,
        mesh=mesh,
        in_specs=placed,
        out_specs=P("group", None, None, "tp"),
        check_vma=False,
    )
```
